256 devices in a mesh: dp: 4 (over x), state: 64 (over y, z, core).
Axes of the slice: x: 4, y: 4, z: 8, core: 2. Of those that a mesh axis runs over, the one named last changes fastest.
Arguments:
- alpha_init: bfloat16 [32, 1024, 1024], P('dp', 'state'), may hold values from 0.099609375 to 4
- tokens: int32 [32, 3], P('dp'), may hold values from 0 to 511
- trans_rows: bfloat16 [1024, 1024], replicated, may hold values from 5e-05 to 1.11, as said below
- trans_cols: bfloat16 [1024, 1024], replicated, may hold values from 5e-05 to 1.11, as said below
- emit_rows: bfloat16 [512, 1024], replicated, may hold values from 0.001 to 1, as said below
- emit_cols: bfloat16 [512, 1024], replicated, may hold values from 0.001 to 1, as said below
- backward: bfloat16 [3, 32, 1024, 1024], P(None, 'dp', None, 'state'), may hold values from 0.2 to 32, as said below
Outputs:
- alpha_final: bfloat16 [32, 1024, 1024], P('dp', 'state')
- counts_rows: float32 [1024, 1024], P(None, ('dp', 'state'))
- counts_cols: float32 [1024, 1024], P(None, ('dp', 'state'))
- loglik: float32 [32], P('dp')
The draws below stay inside these ranges and needn't reach their ends.
Inputs may be any that keep to these rules, and one draw needn't show every extreme that they name: `trans_rows`: positive transition weights. `trans_cols`: positive transition weights. `emit_rows`: positive emission weights. `emit_cols`: positive emission weights. Positive backward weights.
All inputs are finite; a program needn't handle non-finite values.
Results may differ from the reference program's by a relative error of at most 0.0046.
Values may be sent and summed in bfloat16 or wider, within the bound.
No kernel may reach another device: no remote copies, remote signals or barrier semaphores. Data moves between devices by JAX's collectives and lax.ppermute only.
A program may use at most 128 MiB of HBM per device.

```python
import math
import jax
import jax.numpy as jnp

K1 = 1024
K2 = 1024
VOCAB = 512
STEPS = 3
SEQ = 32
N_STATE = 64


def build_factor(key, width, marker):
    base = jax.random.fold_in(key, marker)
    key_floor, key_main, key_side, key_mainval, key_sideval = jax.random.split(base, 5)
    logs = jax.random.uniform(key_floor, (width, width), jnp.float32, math.log(5e-05), math.log(0.003))
    floor_part = jnp.exp(logs)
    main_value = jax.random.uniform(key_mainval, (width, 1), jnp.float32, 0.4, 0.7)
    side_value = jax.random.uniform(key_sideval, (width, 1), jnp.float32, 0.1, 0.3)
    main_order = jax.random.permutation(key_main, width)
    side_order = jax.random.permutation(key_side, width)
    columns = jnp.arange(width, dtype=jnp.int32)
    main_onehot = (main_order.astype(jnp.int32)[:, None] == columns[None, :]).astype(jnp.float32)
    side_onehot = (side_order.astype(jnp.int32)[:, None] == columns[None, :]).astype(jnp.float32)
    return floor_part + main_value * main_onehot + side_value * side_onehot


def build_emission(key, width, marker):
    base = jax.random.fold_in(key, marker)
    key_low = jax.random.fold_in(base, 1)
    logs = jax.random.uniform(key_low, (VOCAB, width), jnp.float32, math.log(0.001), 0.0)
    values = jnp.exp(logs)
    return values


def draw_trans_rows(key, part):
    return build_factor(key, K1, 101).astype(jnp.bfloat16)


def draw_trans_cols(key, part):
    return build_factor(key, K2, 202).astype(jnp.bfloat16)


def draw_emit_rows(key, part):
    return build_emission(key, K1, 404).astype(jnp.bfloat16)


def draw_emit_cols(key, part):
    return build_emission(key, K2, 505).astype(jnp.bfloat16)


def draw_backward(key, part):
    base = jax.random.fold_in(key, 303)
    key_vals, key_pair = jax.random.split(base, 2)
    logs = jax.random.uniform(key_vals, (STEPS, SEQ, K1, K2), jnp.float32, math.log(0.2), math.log(2.0))
    values = jnp.exp(logs)
    pairing = jax.random.permutation(key_pair, N_STATE).astype(jnp.int32)
    row_block = jnp.arange(K1, dtype=jnp.int32) // (K1 // N_STATE)
    col_block = jnp.arange(K2, dtype=jnp.int32) // (K2 // N_STATE)
    paired = (pairing[col_block][None, :] == row_block[:, None]).astype(jnp.float32)
    boost = 1.0 + 15.0 * paired
    return (values * boost[None, None, :, :]).astype(jnp.bfloat16)


def plant(drawn, rng, smallest, largest):
    spot = [jax.random.randint(jax.random.fold_in(rng, axis), (), 0, length) for axis, length in enumerate(drawn.shape)]
    main_axis = drawn.shape.index(max(drawn.shape))
    neighbour = spot[:main_axis] + [(spot[main_axis] + 1) % drawn.shape[main_axis]] + spot[main_axis + 1:]
    return drawn.at[tuple(spot)].set(smallest).at[tuple(neighbour)].set(largest)


def levels(own_key, shape, cuts, smallest, largest):
    gain, own = 1.0, jax.random.fold_in(own_key, 6)
    for position, parts in cuts:
        draws = jnp.exp(jax.random.uniform(jax.random.fold_in(own, position), (parts,), jnp.float32, smallest / len(cuts), largest / len(cuts)))
        gain = gain * jnp.repeat(draws, shape[position] // parts).reshape([-1 if axis == position else 1 for axis in range(len(shape))])
    return gain


def setup_inputs(seed: int = 0) -> dict:
    seeds = jax.random.split(jax.random.key(seed), 8)
    alpha_init = jnp.clip(jnp.exp(math.log(4.0) - 3.6927934 * jax.random.uniform(seeds[0], (SEQ, K1, K2), jnp.float32) ** levels(seeds[0], (SEQ, K1, K2), ((0, 4), (1, 64)), -0.2, 0.2)), 0.099609375, 4.0).astype(jnp.bfloat16)
    tokens = plant(jax.random.randint(seeds[1], (SEQ, STEPS), 0, VOCAB), jax.random.fold_in(seeds[1], 1), 0, VOCAB - 1).astype(jnp.int32)
    trans_rows = draw_trans_rows(jax.random.fold_in(seeds[7], 71), 0)
    trans_cols = draw_trans_cols(jax.random.fold_in(seeds[7], 71), 0)
    emit_rows = draw_emit_rows(jax.random.fold_in(seeds[7], 71), 0)
    emit_cols = draw_emit_cols(jax.random.fold_in(seeds[7], 71), 0)
    backward = draw_backward(jax.random.fold_in(seeds[7], 71), 0)
    return dict(alpha_init=alpha_init, tokens=tokens, trans_rows=trans_rows, trans_cols=trans_cols, emit_rows=emit_rows, emit_cols=emit_cols, backward=backward)


def reference(alpha_init, tokens, trans_rows, trans_cols, emit_rows, emit_cols, backward):
    f32 = jnp.float32
    alpha = alpha_init
    rows_f = trans_rows.astype(f32)
    cols_f = trans_cols.astype(f32)
    sums_rows = jnp.zeros((K1, K1), f32)
    sums_cols = jnp.zeros((K2, K2), f32)
    loglik = jnp.zeros((SEQ,), f32)
    for step in range(STEPS):
        tok = tokens[:, step]
        first = emit_rows[tok].astype(f32)
        second = emit_cols[tok].astype(f32)
        mixed = jnp.einsum("sij,jk->sik", alpha.astype(f32), cols_f).astype(jnp.bfloat16)
        moved = jnp.einsum("sik,il->slk", mixed.astype(f32), rows_f)
        emission = first[:, :, None] * second[:, None, :]
        scaled = moved * emission
        norm = jnp.sum(scaled, axis=(1, 2)) / (K1 * K2)
        weight = (emission * backward[step].astype(f32) / norm[:, None, None]).astype(jnp.bfloat16)
        pulled = jnp.einsum("il,slk->sik", rows_f, weight.astype(f32)).astype(jnp.bfloat16)
        sums_rows = sums_rows + jnp.einsum("sik,slk->il", mixed.astype(f32), weight.astype(f32))
        sums_cols = sums_cols + jnp.einsum("sij,sik->jk", alpha.astype(f32), pulled.astype(f32))
        loglik = loglik + jnp.log(norm)
        alpha = (scaled / norm[:, None, None]).astype(jnp.bfloat16)
    counts_rows = rows_f * sums_rows / (SEQ * STEPS)
    counts_cols = cols_f * sums_cols / (SEQ * STEPS)
    return (alpha, counts_rows, counts_cols, loglik)
```

```python
import jax
import jax.numpy as jnp
from jax import lax
from jax.experimental import pallas as pl
from jax.experimental.pallas import tpu as pltpu
from jax.sharding import PartitionSpec as P

STEPS = 3
F32 = jnp.float32
BF16 = jnp.bfloat16
SEQ_DEV = 8
PART = 16
ROWS = SEQ_DEV * PART
WIDTH = 1024
PEERS = WIDTH // PART
VMEM = 48 * 2**20


def iota(shape, dim):
    return lax.broadcasted_iota(jnp.int32, shape, dim)


def dot(a, b):
    return lax.dot_general(a, b, (((1,), (0,)), ((), ())), preferred_element_type=F32)


def dot_nt(a, b):
    return lax.dot_general(a, b, (((1,), (1,)), ((), ())), preferred_element_type=F32)


def dot_tn(a, b):
    return lax.dot_general(a, b, (((0,), (0,)), ((), ())), preferred_element_type=F32)


def pick(tok_ref, emit_ref):
    hot = [
        (tok_ref[:, t : t + 1] == iota((SEQ_DEV, emit_ref.shape[0]), 1)).astype(F32)
        for t in range(STEPS)
    ]
    return dot(jnp.concatenate(hot, axis=0).astype(BF16), emit_ref[...])


def step_of(v, t):
    return v[t * SEQ_DEV : (t + 1) * SEQ_DEV]


def spread(v):
    n = v.shape[-1]
    return jnp.broadcast_to(v[:, None, :], (SEQ_DEV, PART, n)).reshape(ROWS, n)


def column_of(v, offset):
    at = offset + (iota((ROWS, WIDTH), 0) & (PART - 1))
    return jnp.sum(jnp.where(iota((ROWS, WIDTH), 1) == at, spread(v), 0.0), axis=1, keepdims=True)


def swap(tiles):
    group = iota((PART, 128), 1) >> 4
    for bit in (1, 2, 4):
        low = (group & bit) == 0
        out = list(tiles)
        for s in range(SEQ_DEV):
            if s & bit == 0:
                a, b = tiles[s], tiles[s + bit]
                out[s] = jnp.where(low, a, pltpu.roll(b, PART * bit, 1))
                out[s + bit] = jnp.where(low, pltpu.roll(a, 128 - PART * bit, 1), b)
        tiles = out
    return tiles


def to_wire(src_ref, dst_ref, row):
    @pl.loop(0, PEERS // SEQ_DEV)
    def _(g):
        lanes = pl.ds(pl.multiple_of(g * 128, 128), 128)
        tiles = swap([src_ref[s * PART : (s + 1) * PART, lanes] for s in range(SEQ_DEV)])
        for s in range(SEQ_DEV):
            dst_ref[g * SEQ_DEV + s, row : row + PART, :] = tiles[s].astype(BF16)


def from_wire(src_ref, row, store):
    @pl.loop(0, PEERS // SEQ_DEV)
    def _(g):
        tiles = swap(
            [src_ref[g * SEQ_DEV + s, row : row + PART, :].astype(F32) for s in range(SEQ_DEV)]
        )
        lanes = pl.ds(pl.multiple_of(g * 128, 128), 128)
        for s in range(SEQ_DEV):
            store(s, lanes, tiles[s])


def inverse_norm(total_ref, t):
    at = STEPS * (iota((ROWS, 128), 0) >> 4) + t
    total = jnp.sum(
        jnp.where(iota((ROWS, 128), 1) == at, total_ref[...], 0.0), axis=1, keepdims=True
    )
    return float(WIDTH * WIDTH) / total


def rows_kernel(alpha_ref, tok_ref, cols_ref, emit_cols_ref, wire_ref, y_ref, sums_ref, x_ref):
    second = pick(tok_ref, emit_cols_ref)
    y = alpha_ref[...]
    sums = jnp.zeros((ROWS, 128), F32)
    for t in range(STEPS):
        x = dot(y, cols_ref[...])
        x_ref[...] = x
        y32 = x * spread(step_of(second, t))
        total = jnp.sum(y32, axis=1, keepdims=True)
        sums = jnp.where(iota((ROWS, 128), 1) == t, total, sums)
        to_wire(x_ref, wire_ref, t * PART)
        if t < STEPS - 1:
            y = y32.astype(BF16)
            y_ref[t] = y
    sums_ref[...] = sums


def weights_kernel(
    tok_ref, rows_ref, cols_ref, emit_rows_ref, emit_cols_ref, back_ref, sums_ref,
    wire_ref, weight_ref, norm_ref, take_rows_ref, take_cols_ref, first_ref, local_ref,
    wt_ref, g_ref,
):
    me = lax.axis_index("state")
    offset = me * PART
    first = pick(tok_ref, emit_rows_ref)
    first_ref[...] = first
    second = pick(tok_ref, emit_cols_ref)
    local = jnp.zeros((ROWS, 128), F32)
    for t in range(STEPS):
        column = column_of(step_of(second, t), offset)
        local = jnp.where(iota((ROWS, 128), 1) == t, column, local)
        w = spread(step_of(first, t)) * column * back_ref[t].astype(F32)
        wt_ref[t * ROWS : (t + 1) * ROWS, :] = w.astype(BF16)
        weight_ref[:, t * ROWS : (t + 1) * ROWS] = w.T.astype(BF16)
    local_ref[...] = local

    pair = (iota((SEQ_DEV, ROWS), 1) >> 4 == iota((SEQ_DEV, ROWS), 0)).astype(BF16)
    factor = [dot_tn(step_of(first, t).astype(BF16), pair) for t in range(STEPS - 1)]
    v = dot_nt(rows_ref[...], wt_ref[...])

    def put(t, value):
        wire_ref[:, t * PART : (t + 1) * PART, :] = value.astype(BF16).reshape(PEERS, PART, ROWS)

    put(0, v[:, :ROWS])
    g_ref[:, :ROWS] = (factor[0] * v[:, ROWS : 2 * ROWS]).astype(BF16)
    g_ref[:, ROWS:] = (factor[1] * v[:, 2 * ROWS :]).astype(BF16)
    v = dot(rows_ref[...], g_ref[...])
    put(1, v[:, :ROWS])
    g_ref[:, :ROWS] = (factor[0] * v[:, ROWS:]).astype(BF16)
    put(2, dot(rows_ref[...], g_ref[:, :ROWS]))

    p = dot_nt(first.astype(BF16), rows_ref[...])
    back = [step_of(p, 0)]
    p = dot_nt((p[SEQ_DEV:] * first[: 2 * SEQ_DEV]).astype(BF16), rows_ref[...])
    back.append(step_of(p, 0))
    p = dot_nt((p[SEQ_DEV:] * first[:SEQ_DEV]).astype(BF16), rows_ref[...])
    back.append(p)
    norm = jnp.zeros((1, 128), F32)
    for t in range(STEPS):
        part = sums_ref[:, t : t + 1] * column_of(back[t], offset)
        at = STEPS * (iota((ROWS, 128), 0) >> 4) + t
        norm = norm + jnp.sum(jnp.where(iota((ROWS, 128), 1) == at, part, 0.0), axis=0, keepdims=True)
    norm_ref[...] = norm

    chip = (lax.axis_index("dp") * PEERS + me) * 4
    hot = (iota((8, WIDTH), 1) == chip + iota((8, WIDTH), 0)) & (iota((8, WIDTH), 0) < 4)
    hot = hot.astype(F32).astype(BF16)
    take_rows_ref[...] = dot_nt(hot, rows_ref[...])
    take_cols_ref[...] = dot_nt(hot, cols_ref[...])


def columns_kernel(
    wire_ref, weight_ref, rows_ref, first_ref, local_ref, total_ref, out_ref, sums_ref, m_ref
):
    first = first_ref[...]

    def x_of(t):
        x = wire_ref[:, t * PART : (t + 1) * PART, :].reshape(WIDTH, ROWS)
        return x.astype(F32).T

    inv = [inverse_norm(total_ref, t) for t in range(STEPS)]
    f0, f1, f2 = (spread(step_of(first, t)) for t in range(STEPS))
    m_ref[:ROWS] = (x_of(0) * inv[0]).astype(BF16)
    x12 = jnp.concatenate([x_of(1).astype(BF16), x_of(2).astype(BF16)], axis=0)
    h = dot(x12, rows_ref[...])
    m_ref[ROWS : 2 * ROWS] = (h[:ROWS] * f0 * inv[1]).astype(BF16)
    h = dot((h[ROWS:] * f0).astype(BF16), rows_ref[...]) * f1
    m_ref[2 * ROWS :] = (h * inv[2]).astype(BF16)
    a = dot(h.astype(BF16), rows_ref[...]) * f2 * (local_ref[:, 2:3] * inv[2])
    out_ref[...] = a.T.astype(BF16).reshape(PEERS, PART, ROWS)

    @pl.loop(0, WIDTH // 256)
    def _(b):
        at = pl.ds(pl.multiple_of(b * 256, 256), 256)
        sums_ref[at, :] = dot(weight_ref[at, :], m_ref[...]).astype(BF16)


def pulled_kernel(wire_ref, alpha_ref, y_ref, total_ref, sums_ref, v_ref, vt_ref, ys_ref):
    for t in range(STEPS):

        def store(s, lanes, tile):
            v_ref[s * PART : (s + 1) * PART, lanes] = tile

        from_wire(wire_ref, t * PART, store)
        vt_ref[:, t * ROWS : (t + 1) * ROWS] = v_ref[...].T.astype(BF16)
        y = alpha_ref[...] if t == 0 else y_ref[t - 1]
        ys_ref[t * ROWS : (t + 1) * ROWS] = (y.astype(F32) * inverse_norm(total_ref, t)).astype(BF16)

    @pl.loop(0, WIDTH // 256)
    def _(b):
        at = pl.ds(pl.multiple_of(b * 256, 256), 256)
        sums_ref[at, :] = dot(vt_ref[at, :], ys_ref[...]).astype(BF16)


def final_kernel(wire_ref, out_ref):
    def store(s, lanes, tile):
        out_ref[s * PART : (s + 1) * PART, lanes] = tile.astype(BF16)

    from_wire(wire_ref, 0, store)


def call(kernel, name, outs, scratch=(), flops=10**9, moved=8 * 10**6):
    return pl.pallas_call(
        kernel,
        name=name,
        out_shape=[jax.ShapeDtypeStruct(s, d) for s, d in outs],
        scratch_shapes=[pltpu.VMEM(s, d) for s, d in scratch],
        compiler_params=pltpu.CompilerParams(vmem_limit_bytes=VMEM),
        cost_estimate=pl.CostEstimate(flops=flops, bytes_accessed=moved, transcendentals=0),
    )


def exchange(x, groups=None, axis="state"):
    return lax.all_to_all(x, axis, 0, 0, axis_index_groups=groups, tiled=True)


def on_device(alpha_init, tokens, trans_rows, trans_cols, emit_rows, emit_cols, backward):
    alpha = alpha_init.reshape(ROWS, WIDTH)
    back = jnp.swapaxes(backward, 2, 3).reshape(STEPS, ROWS, WIDTH)
    wire = (PEERS, STEPS * PART, ROWS)

    x_wire, y, sums = call(
        rows_kernel, "rows",
        [(wire, BF16), ((STEPS - 1, ROWS, WIDTH), BF16), ((ROWS, 128), F32)],
        [((ROWS, WIDTH), F32)],
    )(alpha, tokens, trans_cols, emit_cols)
    x_got = exchange(x_wire)

    v_wire, weight, norm, take_rows, take_cols, first, local = call(
        weights_kernel, "weights",
        [
            (wire, BF16), ((WIDTH, STEPS * ROWS), BF16), ((1, 128), F32), ((8, WIDTH), F32),
            ((8, WIDTH), F32), ((STEPS * SEQ_DEV, WIDTH), F32), ((ROWS, 128), F32),
        ],
        [((STEPS * ROWS, WIDTH), BF16), ((WIDTH, 2 * ROWS), BF16)],
    )(tokens, trans_rows, trans_cols, emit_rows, emit_cols, back, sums)
    norms = exchange(jnp.broadcast_to(norm[None], (PEERS, 1, 128)))
    v_got = exchange(v_wire)
    total = jnp.sum(norms, axis=0)

    a_wire, sums_rows = call(
        columns_kernel, "columns",
        [((PEERS, PART, ROWS), BF16), ((WIDTH, WIDTH), BF16)],
        [((STEPS * ROWS, WIDTH), BF16)],
    )(x_got, weight, trans_rows, first, local, total)
    a_got = exchange(a_wire)

    (sums_cols,) = call(
        pulled_kernel, "pulled", [((WIDTH, WIDTH), BF16)],
        [((ROWS, WIDTH), F32), ((WIDTH, STEPS * ROWS), BF16), ((STEPS * ROWS, WIDTH), BF16)],
    )(v_got, alpha, y, total)

    ny, nz = 4, 8
    core = lax.axis_index("state") & 1
    pairs = [(i, i ^ 1) for i in range(PEERS)]
    group_y = [[(b * nz + z) * 2 + c for b in range(ny)] for z in range(nz) for c in range(2)]
    group_z = [[(b * nz + z) * 2 + c for z in range(nz)] for b in range(ny) for c in range(2)]
    keep = jnp.where(core == 0, sums_rows, sums_cols)
    give = jnp.where(core == 0, sums_cols, sums_rows)
    part = keep.astype(F32) + lax.ppermute(give, "state", pairs).astype(F32)
    part = exchange(part.astype(BF16).reshape(4, 256, WIDTH), axis="dp")
    part = jnp.sum(part.astype(F32), axis=0)
    part = exchange(part.astype(BF16).reshape(ny, 64, WIDTH), group_y)
    part = jnp.sum(part.astype(F32), axis=0)
    part = exchange(part.astype(BF16).reshape(nz, 8, WIDTH), group_z)
    part = jnp.sum(part.astype(F32), axis=0)
    mine = jnp.where(core == 0, part[:4], part[4:])
    other = lax.ppermute(jnp.where(core == 0, part[4:], part[:4]), "state", pairs)
    scale = 1.0 / (SEQ_DEV * 4 * STEPS)
    counts_rows = jnp.where(core == 0, mine, other) * take_rows[:4] * scale
    counts_cols = jnp.where(core == 0, other, mine) * take_cols[:4] * scale

    (alpha_final,) = call(final_kernel, "final", [((ROWS, WIDTH), BF16)])(a_got)
    loglik = jnp.log(total[0, 2 : 3 * SEQ_DEV : 3] / (WIDTH * WIDTH))
    return (
        alpha_final.reshape(SEQ_DEV, PART, WIDTH),
        counts_rows.T,
        counts_cols.T,
        loglik,
    )


def solution(mesh):
    return jax.shard_map(
        on_device,
        mesh=mesh,
        in_specs=(
            P("dp", "state", None),
            P("dp", None),
            P(),
            P(),
            P(),
            P(),
            P(None, "dp", None, "state"),
        ),
        out_specs=(
            P("dp", "state", None),
            P(None, ("dp", "state")),
            P(None, ("dp", "state")),
            P("dp"),
        ),
        check_vma=False,
    )
```

```python
import jax
import jax.numpy as jnp
from jax import lax
from jax.experimental import pallas as pl
from jax.experimental.pallas import tpu as pltpu
from jax.sharding import PartitionSpec as P

STEPS = 3
F32 = jnp.float32
BF16 = jnp.bfloat16
SEQ_DEV = 8
PART = 16
ROWS = SEQ_DEV * PART
WIDTH = 1024
PEERS = WIDTH // PART
VMEM = 24 * 2**20
ALONE = 60 * 2**20
NORM = 2 * STEPS * PART
WIRE = NORM + 8


def iota(shape, dim):
    return lax.broadcasted_iota(jnp.int32, shape, dim)


def dot(a, b):
    return lax.dot_general(a, b, (((1,), (0,)), ((), ())), preferred_element_type=F32)


def dot_nt(a, b):
    return lax.dot_general(a, b, (((1,), (1,)), ((), ())), preferred_element_type=F32)


def dot_tn(a, b):
    return lax.dot_general(a, b, (((0,), (0,)), ((), ())), preferred_element_type=F32)


def pick(tok_ref, emit_ref):
    rows = emit_ref.shape[0]
    hot = [
        (tok_ref[t : t + 1, :] == iota((rows, SEQ_DEV), 0)).astype(F32) for t in range(STEPS)
    ]
    return dot_tn(jnp.concatenate(hot, axis=1).astype(BF16), emit_ref[...])


def step_of(v, t):
    return v[t * SEQ_DEV : (t + 1) * SEQ_DEV]


def spread(v):
    n = v.shape[-1]
    return jnp.broadcast_to(v[:, None, :], (SEQ_DEV, PART, n)).reshape(ROWS, n)


def column_of(v, offset):
    at = offset + (iota((ROWS, WIDTH), 0) & (PART - 1))
    return jnp.sum(jnp.where(iota((ROWS, WIDTH), 1) == at, spread(v), 0.0), axis=1, keepdims=True)


def swap(tiles):
    group = iota((PART, 128), 1) >> 4
    for bit in (1, 2, 4):
        low = (group & bit) == 0
        out = list(tiles)
        for s in range(SEQ_DEV):
            if s & bit == 0:
                a, b = tiles[s], tiles[s + bit]
                out[s] = jnp.where(low, a, pltpu.roll(b, PART * bit, 1))
                out[s + bit] = jnp.where(low, pltpu.roll(a, 128 - PART * bit, 1), b)
        tiles = out
    return tiles


def to_wire(src_ref, dst_ref, row):
    for g in range(PEERS // SEQ_DEV):
        lanes = slice(g * 128, (g + 1) * 128)
        tiles = swap([src_ref[s * PART : (s + 1) * PART, lanes] for s in range(SEQ_DEV)])
        for s in range(SEQ_DEV):
            dst_ref[g * SEQ_DEV + s, row : row + PART, :] = tiles[s].astype(BF16)


def from_wire(src_ref, row, store):
    for g in range(PEERS // SEQ_DEV):
        tiles = swap(
            [src_ref[g * SEQ_DEV + s, row : row + PART, :].astype(F32) for s in range(SEQ_DEV)]
        )
        lanes = slice(g * 128, (g + 1) * 128)
        for s in range(SEQ_DEV):
            store(s, lanes, tiles[s])


def state_index():
    return (lax.axis_index("y") * 8 + lax.axis_index("z")) * 2 + lax.axis_index("core")


def total_of(wire_ref):
    return jnp.sum(jnp.sum(wire_ref[:, NORM:WIRE, :].astype(F32), axis=0), axis=0, keepdims=True)


def inverse_norm(totals, t):
    at = STEPS * (iota((ROWS, 128), 0) >> 4) + t
    total = jnp.sum(jnp.where(iota((ROWS, 128), 1) == at, totals, 0.0), axis=1, keepdims=True)
    return float(WIDTH * WIDTH) / total


def send_kernel(
    tok_ref, alpha_hbm, rows_hbm, cols_hbm, emit_rows_hbm, emit_cols_hbm, back_hbm,
    wire_hbm, y_hbm, alpha_ref, rows_ref, cols_ref, emit_rows_ref, emit_cols_ref, back_ref,
    wire_ref, y_ref, x_ref, wt_ref, g_ref, in_sem, out_sem,
):
    pairs = [
        (emit_cols_hbm, emit_cols_ref), (alpha_hbm, alpha_ref), (cols_hbm, cols_ref),
        (emit_rows_hbm, emit_rows_ref), (back_hbm, back_ref), (rows_hbm, rows_ref),
    ]
    loads = [pltpu.make_async_copy(a, b, in_sem.at[n]) for n, (a, b) in enumerate(pairs)]
    for load in loads:
        load.start()
    stores = []

    def keep(src, dst):
        store = pltpu.make_async_copy(src, dst, out_sem.at[len(stores)])
        store.start()
        stores.append(store)

    def send(n, value):
        x_ref[...] = value
        at = slice(n * PART, (n + 1) * PART)
        to_wire(x_ref, wire_ref, n * PART)
        keep(wire_ref.at[:, at, :], wire_hbm.at[:, at, :])

    offset = state_index() * PART
    loads[0].wait()
    second = pick(tok_ref, emit_cols_ref)
    loads[1].wait()
    loads[2].wait()
    y = alpha_ref[...]
    sums = []
    for t in range(STEPS):
        x = dot(y, cols_ref[...])
        y32 = x * spread(step_of(second, t))
        sums.append(jnp.sum(y32, axis=1, keepdims=True))
        if t < STEPS - 1:
            y = y32.astype(BF16)
            y_ref[t] = y
        send(t, x)
    keep(y_ref, y_hbm)

    loads[3].wait()
    first = pick(tok_ref, emit_rows_ref)
    f0, f1 = (spread(step_of(first, t)) for t in range(2))
    loads[4].wait()
    for t in range(STEPS):
        column = column_of(step_of(second, t), offset)
        w = spread(step_of(first, t)) * column * back_ref[t].astype(F32)
        wt_ref[t * ROWS : (t + 1) * ROWS, :] = w.astype(BF16)
    wt_ref[STEPS * ROWS :, :] = first.astype(BF16)
    loads[5].wait()
    v = dot_nt(wt_ref[...], rows_ref[...])
    ends = [v[3 * ROWS : 3 * ROWS + 8]]
    g_ref[:ROWS] = (v[ROWS : 2 * ROWS] * f0).astype(BF16)
    g_ref[ROWS : 2 * ROWS] = (v[2 * ROWS : 3 * ROWS] * f1).astype(BF16)
    g_ref[2 * ROWS :] = (v[3 * ROWS + 8 :] * first[:16]).astype(BF16)
    send(STEPS, v[:ROWS])
    v = dot_nt(g_ref[...], rows_ref[...])
    ends.append(v[2 * ROWS : 2 * ROWS + 8])
    g_ref[:ROWS] = (v[ROWS : 2 * ROWS] * f0).astype(BF16)
    tail = (v[2 * ROWS + 8 :] * first[:8]).astype(BF16)
    g_ref[ROWS : ROWS + 16] = jnp.concatenate([tail, tail], axis=0)
    send(STEPS + 1, v[:ROWS])
    v = dot_nt(g_ref[: ROWS + 16], rows_ref[...])
    ends.append(v[ROWS : ROWS + 8])
    send(STEPS + 2, v[:ROWS])

    norm = jnp.zeros((1, 128), F32)
    for t in range(STEPS):
        part = sums[t] * column_of(ends[t], offset)
        at = STEPS * (iota((ROWS, 128), 0) >> 4) + t
        norm = norm + jnp.sum(jnp.where(iota((ROWS, 128), 1) == at, part, 0.0), axis=0, keepdims=True)
    high = norm.astype(BF16).astype(F32)
    middle = (norm - high).astype(BF16).astype(F32)
    low = norm - high - middle
    row = iota((8, 128), 0)
    parts = jnp.where(row == 0, high, jnp.where(row == 1, middle, jnp.where(row == 2, low, 0.0)))
    wire_ref[:, NORM:WIRE, :] = jnp.broadcast_to(parts.astype(BF16)[None], (PEERS, 8, 128))
    keep(wire_ref.at[:, NORM:WIRE, :], wire_hbm.at[:, NORM:WIRE, :])
    for store in stores:
        store.wait()


def to_row(column):
    return jnp.sum(
        jnp.where(iota((128, 128), 0) == iota((128, 128), 1), column, 0.0), axis=0, keepdims=True
    )


def local_kernel(
    tok_ref, rows_ref, cols_ref, emit_rows_ref, emit_cols_ref, back_ref,
    weight_ref, turned_ref, factor_ref, local_ref, take_rows_ref, take_cols_ref,
):
    me = state_index()
    first = pick(tok_ref, emit_rows_ref)
    second = pick(tok_ref, emit_cols_ref)
    pair = (iota((SEQ_DEV, ROWS), 1) >> 4 == iota((SEQ_DEV, ROWS), 0)).astype(F32).astype(BF16)
    for t in range(STEPS):
        column = column_of(step_of(second, t), me * PART)
        w = spread(step_of(first, t)) * column * back_ref[t].astype(F32)
        weight_ref[:, t * ROWS : (t + 1) * ROWS] = w.T.astype(BF16)
        factor_ref[t] = dot_tn(step_of(first, t).astype(BF16), pair).astype(BF16)
        if t == STEPS - 1:
            local_ref[...] = to_row(column)

    @pl.loop(0, WIDTH // 128)
    def _(b):
        at = pl.ds(pl.multiple_of(b * 128, 128), 128)
        turned_ref[at, :] = rows_ref[:, at].astype(F32).T.astype(BF16)

    mine = (lax.axis_index("dp") * PEERS + me) * 4
    hot = (iota((8, WIDTH), 1) == mine + iota((8, WIDTH), 0)) & (iota((8, WIDTH), 0) < 4)
    hot = hot.astype(F32).astype(BF16)
    take_rows_ref[...] = dot_nt(hot, rows_ref[...])
    take_cols_ref[...] = dot_nt(hot, cols_ref[...])


def counts_kernel(
    wire_hbm, y_hbm, alpha_hbm, turned_hbm, factor_hbm, weight_hbm, local_ref,
    out_hbm, keep_hbm, give_hbm, total_ref,
    wire_ref, y_ref, alpha_ref, turned_ref, factor_ref, weight_ref, out_ref,
    rows_ref, cols_ref, ys_ref, m_ref, in_sem, out_sem,
):
    pairs = [
        (wire_hbm, wire_ref), (y_hbm, y_ref), (alpha_hbm, alpha_ref), (turned_hbm, turned_ref),
        (factor_hbm, factor_ref), (weight_hbm, weight_ref),
    ]
    loads = [pltpu.make_async_copy(a, b, in_sem.at[n]) for n, (a, b) in enumerate(pairs)]
    for load in loads:
        load.start()
    for load in loads[:3]:
        load.wait()
    core = lax.axis_index("core")
    keep_rows = pltpu.make_async_copy(rows_ref, keep_hbm, out_sem.at[1])
    give_rows = pltpu.make_async_copy(rows_ref, give_hbm, out_sem.at[1])
    keep_cols = pltpu.make_async_copy(cols_ref, keep_hbm, out_sem.at[2])
    give_cols = pltpu.make_async_copy(cols_ref, give_hbm, out_sem.at[2])

    totals = total_of(wire_ref)
    total_ref[...] = totals
    inverse = [inverse_norm(totals, t) for t in range(STEPS)]
    inv = [to_row(i) for i in inverse]
    for t in range(STEPS):
        y = alpha_ref[...] if t == 0 else y_ref[t - 1]
        ys_ref[t * ROWS : (t + 1) * ROWS] = (y.astype(F32) * inverse[t]).astype(BF16)
    for b in range(4):
        peers = slice(b * 16, (b + 1) * 16)
        v = jnp.concatenate(
            [
                wire_ref[peers, (STEPS + t) * PART : (STEPS + t + 1) * PART, :].reshape(256, ROWS)
                for t in range(STEPS)
            ],
            axis=1,
        )
        cols_ref[b * 256 : (b + 1) * 256, :] = dot(v, ys_ref[...]).astype(BF16)

    @pl.when(core == 0)
    def _():
        give_cols.start()

    @pl.when(core == 1)
    def _():
        keep_cols.start()

    def x_of(t):
        return wire_ref[:, t * PART : (t + 1) * PART, :].reshape(WIDTH, ROWS)

    m_ref[:, :ROWS] = (x_of(0).astype(F32) * inv[0]).astype(BF16)
    loads[3].wait()
    loads[4].wait()
    f0, f1, f2 = (factor_ref[t].astype(F32) for t in range(STEPS))
    h = dot(turned_ref[...], jnp.concatenate([x_of(1), x_of(2)], axis=1))
    m_ref[:, ROWS : 2 * ROWS] = (h[:, :ROWS] * f0 * inv[1]).astype(BF16)
    h = dot(turned_ref[...], (h[:, ROWS:] * f0).astype(BF16)) * f1
    m_ref[:, 2 * ROWS :] = (h * inv[2]).astype(BF16)
    a = dot(turned_ref[...], h.astype(BF16)) * f2 * (local_ref[...] * inv[2])
    out_ref[...] = a.astype(BF16).reshape(PEERS, PART, ROWS)
    send = pltpu.make_async_copy(out_ref, out_hbm, out_sem.at[0])
    send.start()
    loads[5].wait()
    for b in range(WIDTH // 256):
        at = slice(b * 256, (b + 1) * 256)
        rows_ref[:, at] = dot_nt(weight_ref[...], m_ref[at, :]).astype(BF16)

    @pl.when(core == 0)
    def _():
        keep_rows.start()
        keep_rows.wait()
        give_cols.wait()

    @pl.when(core == 1)
    def _():
        give_rows.start()
        give_rows.wait()
        keep_cols.wait()

    send.wait()


def pair_kernel(keep_ref, got_ref, *outs):
    half = WIDTH // 2
    x, y = lax.axis_index("dp"), lax.axis_index("y")

    def piece(at, lanes):
        return (keep_ref[at, lanes].astype(F32) + got_ref[at, lanes].astype(F32)).astype(BF16)

    for d in range(4):
        at = pl.ds(pl.multiple_of(((x + d) & 3) * 256, 256), 256)
        outs[d][...] = piece(at, slice(0, half))
        for b in range(4):
            at = pl.ds(pl.multiple_of(b * 256 + ((y + d) & 3) * 64, 64), 64)
            outs[4 + d][b * 64 : (b + 1) * 64, :] = piece(at, slice(half, WIDTH))


def plane_kernel(*refs):
    ins, outs, (sum_ref,) = refs[:8], refs[8:16], refs[16:]
    for side in range(2):
        at = lax.axis_index("y" if side == 0 else "dp")
        group = ins[4 * side : 4 * side + 4]
        sum_ref[...] = sum(r[...].astype(F32) for r in group)
        for d in range(4):
            rows = pl.ds(pl.multiple_of(((at + d) & 3) * 64, 64), 64)
            outs[4 * side + d][...] = sum_ref[rows, :].astype(BF16)


def line_kernel(*refs):
    ins, out_ref = refs[:8], refs[8]
    half = WIDTH // 2
    for side in range(2):
        group = ins[4 * side : 4 * side + 4]
        total = sum(r[...].astype(F32) for r in group).astype(BF16)
        out_ref[:, side * half : (side + 1) * half] = total


def final_kernel(wire_ref, out_ref):
    def store(s, lanes, tile):
        out_ref[s * PART : (s + 1) * PART, lanes] = tile.astype(BF16)

    from_wire(wire_ref, 0, store)


def call(kernel, name, outs, scratch=(), flops=10**9, moved=8 * 10**6, limit=VMEM, specs=None):
    return pl.pallas_call(
        kernel,
        name=name,
        out_shape=[jax.ShapeDtypeStruct(s, d) for s, d in outs],
        scratch_shapes=[s if hasattr(s, "dtype") else pltpu.VMEM(*s) for s in scratch],
        compiler_params=pltpu.CompilerParams(vmem_limit_bytes=limit),
        cost_estimate=pl.CostEstimate(flops=flops, bytes_accessed=moved, transcendentals=0),
        **(specs or {}),
    )


def ring(x, axis, d, n=4):
    return lax.ppermute(x, axis, [(i, (i + d) % n) for i in range(n)])


def spread_out(pieces, axis):
    far, right, left = (ring(pieces[d], axis, d) for d in (2, 1, 3))
    return [pieces[0], right, far, left]


def on_device(alpha_init, tokens, trans_rows, trans_cols, emit_rows, emit_cols, backward):
    alpha = alpha_init.reshape(ROWS, WIDTH)
    back = jnp.swapaxes(backward, 2, 3).reshape(STEPS, ROWS, WIDTH)
    tok = tokens.T
    half = WIDTH // 2
    state = ("y", "z", "core")

    hbm = pl.BlockSpec(memory_space=pltpu.HBM)
    wire_shape, y_shape = (PEERS, WIRE, ROWS), (STEPS - 1, ROWS, WIDTH)
    square, emit_shape = (WIDTH, WIDTH), emit_rows.shape
    wire, y = call(
        send_kernel, "send", [(wire_shape, BF16), (y_shape, BF16)],
        [
            ((ROWS, WIDTH), BF16), (square, BF16), (square, BF16), (emit_shape, BF16),
            (emit_shape, BF16), ((STEPS, ROWS, WIDTH), BF16), (wire_shape, BF16),
            (y_shape, BF16), ((ROWS, WIDTH), F32), ((STEPS * (ROWS + 8), WIDTH), BF16),
            ((2 * (ROWS + 8), WIDTH), BF16), pltpu.SemaphoreType.DMA((6,)),
            pltpu.SemaphoreType.DMA((8,)),
        ],
        limit=ALONE,
        specs=dict(
            in_specs=[pl.BlockSpec(memory_space=pltpu.VMEM)] + [hbm] * 6, out_specs=[hbm] * 2
        ),
    )(tok, alpha, trans_rows, trans_cols, emit_rows, emit_cols, back)
    got = lax.all_to_all(wire, state, 0, 0, tiled=True)

    weight, turned, factor, local, take_rows, take_cols = call(
        local_kernel, "local",
        [
            ((WIDTH, STEPS * ROWS), BF16), (square, BF16), ((STEPS, WIDTH, ROWS), BF16),
            ((1, ROWS), F32), ((8, WIDTH), F32), ((8, WIDTH), F32),
        ],
        limit=ALONE,
    )(tok, trans_rows, trans_cols, emit_rows, emit_cols, back)

    a_shape = (PEERS, PART, ROWS)
    a_wire, keep, give, total = call(
        counts_kernel, "counts",
        [(a_shape, BF16), (square, BF16), (square, BF16), ((1, 128), F32)],
        [
            (wire_shape, BF16), (y_shape, BF16), ((ROWS, WIDTH), BF16), (square, BF16),
            ((STEPS, WIDTH, ROWS), BF16), ((WIDTH, STEPS * ROWS), BF16), (a_shape, BF16),
            (square, BF16), (square, BF16), ((STEPS * ROWS, WIDTH), BF16),
            ((WIDTH, STEPS * ROWS), BF16), pltpu.SemaphoreType.DMA((6,)),
            pltpu.SemaphoreType.DMA((3,)),
        ],
        limit=ALONE,
        specs=dict(
            in_specs=[hbm] * 6 + [pl.BlockSpec(memory_space=pltpu.VMEM)],
            out_specs=[hbm] * 3 + [pl.BlockSpec(memory_space=pltpu.VMEM)],
        ),
    )(got, y, alpha, turned, factor, weight, local)

    core = lax.axis_index("core")
    swap_cores = [(0, 1), (1, 0)]
    pieces = call(pair_kernel, "pair", [((256, half), BF16)] * 8)(
        keep, lax.ppermute(give, "core", swap_cores)
    )
    a_wire, *pieces = lax.optimization_barrier((a_wire, *pieces))
    parts = spread_out(pieces[:4], "dp") + spread_out(pieces[4:], "y")
    a_got = lax.all_to_all(a_wire, state, 0, 0, tiled=True)
    pieces = call(plane_kernel, "plane", [((64, half), BF16)] * 8, [((256, half), F32)])(*parts)
    a_got, *pieces = lax.optimization_barrier((a_got, *pieces))
    parts = spread_out(pieces[:4], "y") + spread_out(pieces[4:], "dp")
    (part,) = call(line_kernel, "line", [((64, WIDTH), BF16)])(*parts)
    (alpha_final,) = call(final_kernel, "final", [((ROWS, WIDTH), BF16)])(a_got)
    part, alpha_final = lax.optimization_barrier((part, alpha_final))
    part = lax.all_to_all(part.reshape(8, 8, WIDTH), "z", 0, 0, tiled=True)
    part = jnp.sum(part.astype(F32), axis=0)
    mine = jnp.where(core == 0, part[:4], part[4:])
    other = lax.ppermute(jnp.where(core == 0, part[4:], part[:4]), "core", swap_cores)
    scale = 1.0 / (SEQ_DEV * 4 * STEPS)
    counts_rows = jnp.where(core == 0, mine, other) * take_rows[:4] * scale
    counts_cols = jnp.where(core == 0, other, mine) * take_cols[:4] * scale

    loglik = jnp.log(total[0, 2 : 3 * SEQ_DEV : 3] / (WIDTH * WIDTH))
    return (
        alpha_final.reshape(SEQ_DEV, PART, WIDTH),
        counts_rows.T,
        counts_cols.T,
        loglik,
    )


def solution(mesh):
    mesh = jax.sharding.Mesh(mesh.devices.reshape(4, 4, 8, 2), ("dp", "y", "z", "core"))
    state = ("y", "z", "core")
    return jax.shard_map(
        on_device,
        mesh=mesh,
        in_specs=(
            P("dp", state, None),
            P("dp", None),
            P(),
            P(),
            P(),
            P(),
            P(None, "dp", None, state),
        ),
        out_specs=(
            P("dp", state, None),
            P(None, ("dp", *state)),
            P(None, ("dp", *state)),
            P("dp"),
        ),
        check_vma=False,
    )
```

```python
import functools

import jax
import jax.numpy as jnp
from jax import lax
from jax.experimental import pallas as pl
from jax.experimental.pallas import tpu as pltpu
from jax.sharding import PartitionSpec as P

STEPS = 3
F32 = jnp.float32
BF16 = jnp.bfloat16
SEQ_DEV = 8
PART = 16
ROWS = SEQ_DEV * PART
WIDTH = 1024
PEERS = WIDTH // PART
VMEM = 24 * 2**20
ALONE = 60 * 2**20
NORM = 2 * STEPS * PART
WIRE = NORM + 8


def iota(shape, dim):
    return lax.broadcasted_iota(jnp.int32, shape, dim)


def dot(a, b):
    return lax.dot_general(a, b, (((1,), (0,)), ((), ())), preferred_element_type=F32)


def dot_nt(a, b):
    return lax.dot_general(a, b, (((1,), (1,)), ((), ())), preferred_element_type=F32)


def dot_tn(a, b):
    return lax.dot_general(a, b, (((0,), (0,)), ((), ())), preferred_element_type=F32)


def pick(tok_ref, emit_ref):
    rows = emit_ref.shape[0]
    hot = [
        (tok_ref[t : t + 1, :] == iota((rows, SEQ_DEV), 0)).astype(F32) for t in range(STEPS)
    ]
    return dot_tn(jnp.concatenate(hot, axis=1).astype(BF16), emit_ref[...])


def step_of(v, t):
    return v[t * SEQ_DEV : (t + 1) * SEQ_DEV]


def spread(v):
    n = v.shape[-1]
    return jnp.broadcast_to(v[:, None, :], (SEQ_DEV, PART, n)).reshape(ROWS, n)


def column_of(v, offset):
    at = offset + (iota((ROWS, WIDTH), 0) & (PART - 1))
    return jnp.sum(jnp.where(iota((ROWS, WIDTH), 1) == at, spread(v), 0.0), axis=1, keepdims=True)


def swap(tiles):
    group = iota((PART, 128), 1) >> 4
    for bit in (1, 2, 4):
        low = (group & bit) == 0
        out = list(tiles)
        for s in range(SEQ_DEV):
            if s & bit == 0:
                a, b = tiles[s], tiles[s + bit]
                out[s] = jnp.where(low, a, pltpu.roll(b, PART * bit, 1))
                out[s + bit] = jnp.where(low, pltpu.roll(a, 128 - PART * bit, 1), b)
        tiles = out
    return tiles


def to_wire(src_ref, dst_ref, row):
    for g in range(PEERS // SEQ_DEV):
        lanes = slice(g * 128, (g + 1) * 128)
        tiles = swap([src_ref[s * PART : (s + 1) * PART, lanes] for s in range(SEQ_DEV)])
        for s in range(SEQ_DEV):
            dst_ref[g * SEQ_DEV + s, row : row + PART, :] = tiles[s].astype(BF16)


def from_wire(src_ref, row, store):
    for g in range(PEERS // SEQ_DEV):
        tiles = swap(
            [src_ref[g * SEQ_DEV + s, row : row + PART, :].astype(F32) for s in range(SEQ_DEV)]
        )
        lanes = slice(g * 128, (g + 1) * 128)
        for s in range(SEQ_DEV):
            store(s, lanes, tiles[s])


def state_index():
    return (lax.axis_index("y") * 8 + lax.axis_index("z")) * 2 + lax.axis_index("core")


def total_of(wire_ref):
    return jnp.sum(jnp.sum(wire_ref[:, NORM:WIRE, :].astype(F32), axis=0), axis=0, keepdims=True)


def inverse_norm(totals, t):
    at = STEPS * (iota((ROWS, 128), 0) >> 4) + t
    total = jnp.sum(jnp.where(iota((ROWS, 128), 1) == at, totals, 0.0), axis=1, keepdims=True)
    return float(WIDTH * WIDTH) / total


def send_kernel(
    tok_ref, alpha_hbm, rows_hbm, cols_hbm, emit_rows_hbm, emit_cols_hbm, back_hbm,
    wire_hbm, y_hbm, alpha_ref, rows_ref, cols_ref, emit_rows_ref, emit_cols_ref, back_ref,
    wire_ref, y_ref, x_ref, wt_ref, g_ref, in_sem, out_sem,
):
    pairs = [
        (emit_cols_hbm, emit_cols_ref), (alpha_hbm, alpha_ref), (cols_hbm, cols_ref),
        (emit_rows_hbm, emit_rows_ref), (back_hbm, back_ref), (rows_hbm, rows_ref),
    ]
    loads = [pltpu.make_async_copy(a, b, in_sem.at[n]) for n, (a, b) in enumerate(pairs)]
    for load in loads:
        load.start()
    stores = []

    def keep(src, dst):
        store = pltpu.make_async_copy(src, dst, out_sem.at[len(stores)])
        store.start()
        stores.append(store)

    def send(n, value):
        x_ref[...] = value
        at = slice(n * PART, (n + 1) * PART)
        to_wire(x_ref, wire_ref, n * PART)
        keep(wire_ref.at[:, at, :], wire_hbm.at[:, at, :])

    offset = state_index() * PART
    loads[0].wait()
    second = pick(tok_ref, emit_cols_ref)
    loads[1].wait()
    loads[2].wait()
    y = alpha_ref[...]
    sums = []
    for t in range(STEPS):
        x = dot(y, cols_ref[...])
        y32 = x * spread(step_of(second, t))
        sums.append(jnp.sum(y32, axis=1, keepdims=True))
        if t < STEPS - 1:
            y = y32.astype(BF16)
            y_ref[t] = y
        send(t, x)
    keep(y_ref, y_hbm)

    loads[3].wait()
    first = pick(tok_ref, emit_rows_ref)
    f0, f1 = (spread(step_of(first, t)) for t in range(2))
    loads[4].wait()
    for t in range(STEPS):
        column = column_of(step_of(second, t), offset)
        w = spread(step_of(first, t)) * column * back_ref[t].astype(F32)
        wt_ref[t * ROWS : (t + 1) * ROWS, :] = w.astype(BF16)
    wt_ref[STEPS * ROWS :, :] = first.astype(BF16)
    loads[5].wait()
    v = dot_nt(wt_ref[...], rows_ref[...])
    ends = [v[3 * ROWS : 3 * ROWS + 8]]
    g_ref[:ROWS] = (v[ROWS : 2 * ROWS] * f0).astype(BF16)
    g_ref[ROWS : 2 * ROWS] = (v[2 * ROWS : 3 * ROWS] * f1).astype(BF16)
    g_ref[2 * ROWS :] = (v[3 * ROWS + 8 :] * first[:16]).astype(BF16)
    send(STEPS, v[:ROWS])
    v = dot_nt(g_ref[...], rows_ref[...])
    ends.append(v[2 * ROWS : 2 * ROWS + 8])
    g_ref[:ROWS] = (v[ROWS : 2 * ROWS] * f0).astype(BF16)
    tail = (v[2 * ROWS + 8 :] * first[:8]).astype(BF16)
    g_ref[ROWS : ROWS + 16] = jnp.concatenate([tail, tail], axis=0)
    send(STEPS + 1, v[:ROWS])
    v = dot_nt(g_ref[: ROWS + 16], rows_ref[...])
    ends.append(v[ROWS : ROWS + 8])
    send(STEPS + 2, v[:ROWS])

    norm = jnp.zeros((1, 128), F32)
    for t in range(STEPS):
        part = sums[t] * column_of(ends[t], offset)
        at = STEPS * (iota((ROWS, 128), 0) >> 4) + t
        norm = norm + jnp.sum(jnp.where(iota((ROWS, 128), 1) == at, part, 0.0), axis=0, keepdims=True)
    high = norm.astype(BF16).astype(F32)
    middle = (norm - high).astype(BF16).astype(F32)
    low = norm - high - middle
    row = iota((8, 128), 0)
    parts = jnp.where(row == 0, high, jnp.where(row == 1, middle, jnp.where(row == 2, low, 0.0)))
    wire_ref[:, NORM:WIRE, :] = jnp.broadcast_to(parts.astype(BF16)[None], (PEERS, 8, 128))
    keep(wire_ref.at[:, NORM:WIRE, :], wire_hbm.at[:, NORM:WIRE, :])
    for store in stores:
        store.wait()


def to_row(column):
    return jnp.sum(
        jnp.where(iota((128, 128), 0) == iota((128, 128), 1), column, 0.0), axis=0, keepdims=True
    )


def local_kernel(
    tok_ref, rows_ref, cols_ref, emit_rows_ref, emit_cols_ref, back_ref,
    weight_ref, turned_ref, factor_ref, local_ref, take_rows_ref, take_cols_ref,
):
    me = state_index()
    first = pick(tok_ref, emit_rows_ref)
    second = pick(tok_ref, emit_cols_ref)
    pair = (iota((SEQ_DEV, ROWS), 1) >> 4 == iota((SEQ_DEV, ROWS), 0)).astype(F32).astype(BF16)
    for t in range(STEPS):
        column = column_of(step_of(second, t), me * PART)
        w = spread(step_of(first, t)) * column * back_ref[t].astype(F32)
        weight_ref[:, t * ROWS : (t + 1) * ROWS] = w.T.astype(BF16)
        factor_ref[t] = dot_tn(step_of(first, t).astype(BF16), pair).astype(BF16)
        if t == STEPS - 1:
            local_ref[...] = to_row(column)

    @pl.loop(0, WIDTH // 128)
    def _(b):
        at = pl.ds(pl.multiple_of(b * 128, 128), 128)
        turned_ref[at, :] = rows_ref[:, at].astype(F32).T.astype(BF16)

    mine = (lax.axis_index("dp") * PEERS + me) * 4
    hot = (iota((8, WIDTH), 1) == mine + iota((8, WIDTH), 0)) & (iota((8, WIDTH), 0) < 4)
    hot = hot.astype(F32).astype(BF16)
    take_rows_ref[...] = dot_nt(hot, rows_ref[...])
    take_cols_ref[...] = dot_nt(hot, cols_ref[...])


def counts_kernel(
    wire_ref, local_ref, y_hbm, alpha_hbm, turned_hbm, factor_hbm, weight_hbm,
    out_hbm, keep_left, keep_right, give_left, give_right, total_ref,
    y_ref, alpha_ref, turned_ref, factor_ref, weight_ref, out_ref, ys_ref, m_ref,
    in_sem, out_sem,
):
    pairs = [
        (y_hbm, y_ref), (alpha_hbm, alpha_ref), (turned_hbm, turned_ref),
        (factor_hbm, factor_ref), (weight_hbm, weight_ref),
    ]
    loads = [pltpu.make_async_copy(a, b, in_sem.at[n]) for n, (a, b) in enumerate(pairs)]
    for load in loads:
        load.start()
    core = lax.axis_index("core")
    half = WIDTH // 2

    def put(own, left, right, at, value):
        value = value.astype(BF16)
        rows, lanes = at
        targets = ((keep_left, keep_right), (give_left, give_right))
        for choice in range(2):

            @pl.when((core == own) if choice == 0 else (core != own))
            def _():
                if left:
                    targets[choice][0][rows, lanes] = value[:, :half] if right else value
                if right:
                    targets[choice][1][rows, lanes] = value[:, half:] if left else value

    totals = total_of(wire_ref)
    total_ref[...] = totals
    inverse = [inverse_norm(totals, t) for t in range(STEPS)]
    inv = [to_row(i) for i in inverse]

    def x_of(t):
        return wire_ref[:, t * PART : (t + 1) * PART, :].reshape(WIDTH, ROWS)

    m_ref[:, :ROWS] = (x_of(0).astype(F32) * inv[0]).astype(BF16)
    loads[0].wait()
    loads[1].wait()
    for t in range(STEPS):
        y = alpha_ref[...] if t == 0 else y_ref[t - 1]
        ys_ref[t * ROWS : (t + 1) * ROWS] = (y.astype(F32) * inverse[t]).astype(BF16)
    for b in range(4):
        peers = slice(b * 16, (b + 1) * 16)
        v = jnp.concatenate(
            [
                wire_ref[peers, (STEPS + t) * PART : (STEPS + t + 1) * PART, :].reshape(256, ROWS)
                for t in range(STEPS)
            ],
            axis=1,
        )
        at = (slice(b * 256, (b + 1) * 256), slice(0, half))
        put(1, True, True, at, dot(v, ys_ref[...]))

    loads[2].wait()
    loads[3].wait()
    f0, f1, f2 = (factor_ref[t].astype(F32) for t in range(STEPS))
    h = dot(turned_ref[...], jnp.concatenate([x_of(1), x_of(2)], axis=1))
    m_ref[:, ROWS : 2 * ROWS] = (h[:, :ROWS] * f0 * inv[1]).astype(BF16)
    h = dot(turned_ref[...], (h[:, ROWS:] * f0).astype(BF16)) * f1
    m_ref[:, 2 * ROWS :] = (h * inv[2]).astype(BF16)
    a = dot(turned_ref[...], h.astype(BF16)) * f2 * (local_ref[...] * inv[2])
    out_ref[...] = a.astype(BF16).reshape(PEERS, PART, ROWS)
    send = pltpu.make_async_copy(out_ref, out_hbm, out_sem)
    send.start()
    loads[4].wait()
    for b in range(4):
        value = dot_nt(weight_ref[...], m_ref[b * 256 : (b + 1) * 256, :])
        at = (slice(0, WIDTH), slice((b & 1) * 256, (b & 1) * 256 + 256))
        put(0, b < 2, b >= 2, at, value)
    send.wait()


def pair_kernel(axis, keep_ref, got_ref, *outs):
    me = lax.axis_index(axis)
    for d in range(4):
        to = (me + d) & 3
        for b in range(4):
            row = to * 256 + b * 64 if axis == "dp" else b * 256 + to * 64
            at = pl.ds(pl.multiple_of(row, 64), 64)
            total = keep_ref[at, :].astype(F32) + got_ref[at, :].astype(F32)
            outs[d][b * 64 : (b + 1) * 64, :] = total.astype(BF16)


def plane_kernel(*refs):
    ins, outs, (sum_ref,) = refs[:8], refs[8:16], refs[16:]
    for side in range(2):
        at = lax.axis_index("y" if side == 0 else "dp")
        group = ins[4 * side : 4 * side + 4]
        sum_ref[...] = sum(r[...].astype(F32) for r in group)
        for d in range(4):
            rows = pl.ds(pl.multiple_of(((at + d) & 3) * 64, 64), 64)
            outs[4 * side + d][...] = sum_ref[rows, :].astype(BF16)


def line_kernel(*refs):
    ins, out_ref = refs[:8], refs[8]
    half = WIDTH // 2
    for side in range(2):
        group = ins[4 * side : 4 * side + 4]
        total = sum(r[...].astype(F32) for r in group).astype(BF16)
        out_ref[:, side * half : (side + 1) * half] = total


def final_kernel(wire_ref, out_ref):
    def store(s, lanes, tile):
        out_ref[s * PART : (s + 1) * PART, lanes] = tile.astype(BF16)

    from_wire(wire_ref, 0, store)


def call(kernel, name, outs, scratch=(), flops=10**9, moved=8 * 10**6, limit=VMEM, specs=None):
    return pl.pallas_call(
        kernel,
        name=name,
        out_shape=[jax.ShapeDtypeStruct(s, d) for s, d in outs],
        scratch_shapes=[s if hasattr(s, "dtype") else pltpu.VMEM(*s) for s in scratch],
        compiler_params=pltpu.CompilerParams(vmem_limit_bytes=limit),
        cost_estimate=pl.CostEstimate(flops=flops, bytes_accessed=moved, transcendentals=0),
        **(specs or {}),
    )


def ring(x, axis, d, n=4):
    return lax.ppermute(x, axis, [(i, (i + d) % n) for i in range(n)])


def spread_out(pieces, axis):
    far, right, left = (ring(pieces[d], axis, d) for d in (2, 1, 3))
    return [pieces[0], right, far, left]


def in_hbm(*arrays):
    return [pltpu.with_memory_space_constraint(v, pltpu.HBM) for v in arrays]


def on_device(alpha_init, tokens, trans_rows, trans_cols, emit_rows, emit_cols, backward):
    alpha = alpha_init.reshape(ROWS, WIDTH)
    back = jnp.swapaxes(backward, 2, 3).reshape(STEPS, ROWS, WIDTH)
    tok = tokens.T
    half = WIDTH // 2
    state = ("y", "z", "core")

    hbm = pl.BlockSpec(memory_space=pltpu.HBM)
    wire_shape, y_shape = (PEERS, WIRE, ROWS), (STEPS - 1, ROWS, WIDTH)
    square, emit_shape = (WIDTH, WIDTH), emit_rows.shape
    wire, y = call(
        send_kernel, "send", [(wire_shape, BF16), (y_shape, BF16)],
        [
            ((ROWS, WIDTH), BF16), (square, BF16), (square, BF16), (emit_shape, BF16),
            (emit_shape, BF16), ((STEPS, ROWS, WIDTH), BF16), (wire_shape, BF16),
            (y_shape, BF16), ((ROWS, WIDTH), F32), ((STEPS * (ROWS + 8), WIDTH), BF16),
            ((2 * (ROWS + 8), WIDTH), BF16), pltpu.SemaphoreType.DMA((6,)),
            pltpu.SemaphoreType.DMA((8,)),
        ],
        limit=ALONE,
        specs=dict(
            in_specs=[pl.BlockSpec(memory_space=pltpu.VMEM)] + [hbm] * 6, out_specs=[hbm] * 2
        ),
    )(tok, alpha, trans_rows, trans_cols, emit_rows, emit_cols, back)
    got = lax.all_to_all(wire, state, 0, 0, tiled=True)

    weight, turned, factor, local, take_rows, take_cols = call(
        local_kernel, "local",
        [
            ((WIDTH, STEPS * ROWS), BF16), (square, BF16), ((STEPS, WIDTH, ROWS), BF16),
            ((1, ROWS), F32), ((8, WIDTH), F32), ((8, WIDTH), F32),
        ],
        limit=ALONE,
    )(tok, trans_rows, trans_cols, emit_rows, emit_cols, back)

    a_shape = (PEERS, PART, ROWS)
    vmem = pl.BlockSpec(memory_space=pltpu.VMEM)
    a_wire, *ends, total = call(
        counts_kernel, "counts",
        [(a_shape, BF16), *[((WIDTH, half), BF16)] * 4, ((1, 128), F32)],
        [
            (y_shape, BF16), ((ROWS, WIDTH), BF16), (square, BF16),
            ((STEPS, WIDTH, ROWS), BF16), ((WIDTH, STEPS * ROWS), BF16), (a_shape, BF16),
            ((STEPS * ROWS, WIDTH), BF16), ((WIDTH, STEPS * ROWS), BF16),
            pltpu.SemaphoreType.DMA((5,)), pltpu.SemaphoreType.DMA(()),
        ],
        limit=40 * 2**20,
        specs=dict(in_specs=[vmem] * 2 + [hbm] * 5, out_specs=[hbm] + [vmem] * 5),
    )(got, local, *in_hbm(y, alpha, turned, factor, weight))
    keep, give = ends[:2], ends[2:]

    core = lax.axis_index("core")
    swap_cores = [(0, 1), (1, 0)]
    parts = []
    for n, axis in enumerate(("dp", "y")):
        got_half = lax.ppermute(give[n], "core", swap_cores)
        pieces = call(functools.partial(pair_kernel, axis), "pair_" + axis, [((256, half), BF16)] * 4)(
            keep[n], got_half
        )
        parts += spread_out(pieces, axis)
    a_wire, parts[1] = lax.optimization_barrier((a_wire, parts[1]))
    a_got = lax.all_to_all(a_wire, state, 0, 0, tiled=True)
    pieces = call(plane_kernel, "plane", [((64, half), BF16)] * 8, [((256, half), F32)])(*parts)
    parts = spread_out(pieces[:4], "y") + spread_out(pieces[4:], "dp")
    (part,) = call(line_kernel, "line", [((64, WIDTH), BF16)])(*parts)
    (alpha_final,) = call(final_kernel, "final", [((ROWS, WIDTH), BF16)])(a_got)
    part = lax.all_to_all(part.reshape(8, 8, WIDTH), "z", 0, 0, tiled=True)
    loglik = jnp.log(total[0, 2 : 3 * SEQ_DEV : 3] / (WIDTH * WIDTH))
    part, alpha_final, loglik = lax.optimization_barrier((part, alpha_final, loglik))
    part = jnp.sum(part.astype(F32), axis=0)
    mine = jnp.where(core == 0, part[:4], part[4:])
    other = lax.ppermute(jnp.where(core == 0, part[4:], part[:4]), "core", swap_cores)
    scale = 1.0 / (SEQ_DEV * 4 * STEPS)
    counts_rows = jnp.where(core == 0, mine, other) * take_rows[:4] * scale
    counts_cols = jnp.where(core == 0, other, mine) * take_cols[:4] * scale

    return (
        alpha_final.reshape(SEQ_DEV, PART, WIDTH),
        counts_rows.T,
        counts_cols.T,
        loglik,
    )


def solution(mesh):
    mesh = jax.sharding.Mesh(mesh.devices.reshape(4, 4, 8, 2), ("dp", "y", "z", "core"))
    state = ("y", "z", "core")
    return jax.shard_map(
        on_device,
        mesh=mesh,
        in_specs=(
            P("dp", state, None),
            P("dp", None),
            P(),
            P(),
            P(),
            P(),
            P(None, "dp", None, state),
        ),
        out_specs=(
            P("dp", state, None),
            P(None, ("dp", *state)),
            P(None, ("dp", *state)),
            P("dp"),
        ),
        check_vma=False,
    )
```

```python
import jax
import jax.numpy as jnp
from jax import lax
from jax.experimental import pallas as pl
from jax.experimental.pallas import tpu as pltpu
from jax.sharding import PartitionSpec as P

STEPS = 3
F32 = jnp.float32
BF16 = jnp.bfloat16
SEQ_DEV = 8
PART = 16
ROWS = SEQ_DEV * PART
WIDTH = 1024
PEERS = WIDTH // PART
VMEM = 24 * 2**20
ALONE = 60 * 2**20
NORM = 2 * STEPS * PART
WIRE = NORM + 8


def iota(shape, dim):
    return lax.broadcasted_iota(jnp.int32, shape, dim)


def dot(a, b):
    return lax.dot_general(a, b, (((1,), (0,)), ((), ())), preferred_element_type=F32)


def dot_nt(a, b):
    return lax.dot_general(a, b, (((1,), (1,)), ((), ())), preferred_element_type=F32)


def dot_tn(a, b):
    return lax.dot_general(a, b, (((0,), (0,)), ((), ())), preferred_element_type=F32)


def pick(tok_ref, emit_ref):
    rows = emit_ref.shape[0]
    hot = [
        (tok_ref[t : t + 1, :] == iota((rows, SEQ_DEV), 0)).astype(F32) for t in range(STEPS)
    ]
    return dot_tn(jnp.concatenate(hot, axis=1).astype(BF16), emit_ref[...])


def step_of(v, t):
    return v[t * SEQ_DEV : (t + 1) * SEQ_DEV]


def spread(v):
    n = v.shape[-1]
    return jnp.broadcast_to(v[:, None, :], (SEQ_DEV, PART, n)).reshape(ROWS, n)


def column_of(v, offset):
    at = offset + (iota((ROWS, WIDTH), 0) & (PART - 1))
    return jnp.sum(jnp.where(iota((ROWS, WIDTH), 1) == at, spread(v), 0.0), axis=1, keepdims=True)


def swap(tiles):
    group = iota((PART, 128), 1) >> 4
    for bit in (1, 2, 4):
        low = (group & bit) == 0
        out = list(tiles)
        for s in range(SEQ_DEV):
            if s & bit == 0:
                a, b = tiles[s], tiles[s + bit]
                out[s] = jnp.where(low, a, pltpu.roll(b, PART * bit, 1))
                out[s + bit] = jnp.where(low, pltpu.roll(a, 128 - PART * bit, 1), b)
        tiles = out
    return tiles


def to_wire(src_ref, dst_ref, row):
    for g in range(PEERS // SEQ_DEV):
        lanes = slice(g * 128, (g + 1) * 128)
        tiles = swap([src_ref[s * PART : (s + 1) * PART, lanes] for s in range(SEQ_DEV)])
        for s in range(SEQ_DEV):
            dst_ref[g * SEQ_DEV + s, row : row + PART, :] = tiles[s].astype(BF16)


def from_wire(src_ref, row, store):
    for g in range(PEERS // SEQ_DEV):
        tiles = swap(
            [src_ref[g * SEQ_DEV + s, row : row + PART, :].astype(F32) for s in range(SEQ_DEV)]
        )
        lanes = slice(g * 128, (g + 1) * 128)
        for s in range(SEQ_DEV):
            store(s, lanes, tiles[s])


def state_index():
    return (lax.axis_index("y") * 8 + lax.axis_index("z")) * 2 + lax.axis_index("core")


def total_of(wire_ref):
    return jnp.sum(jnp.sum(wire_ref[:, NORM:WIRE, :].astype(F32), axis=0), axis=0, keepdims=True)


def inverse_norm(totals, t):
    at = STEPS * (iota((ROWS, 128), 0) >> 4) + t
    total = jnp.sum(jnp.where(iota((ROWS, 128), 1) == at, totals, 0.0), axis=1, keepdims=True)
    return float(WIDTH * WIDTH) / total


def send_kernel(
    tok_ref, alpha_hbm, rows_hbm, cols_hbm, emit_rows_hbm, emit_cols_hbm, back_hbm,
    wire_hbm, y_hbm, alpha_ref, rows_ref, cols_ref, emit_rows_ref, emit_cols_ref, back_ref,
    wire_ref, y_ref, x_ref, wt_ref, g_ref, in_sem, out_sem,
):
    pairs = [
        (emit_cols_hbm, emit_cols_ref), (alpha_hbm, alpha_ref), (cols_hbm, cols_ref),
        (emit_rows_hbm, emit_rows_ref), (back_hbm, back_ref), (rows_hbm, rows_ref),
    ]
    loads = [pltpu.make_async_copy(a, b, in_sem.at[n]) for n, (a, b) in enumerate(pairs)]
    for load in loads:
        load.start()
    stores = []

    def keep(src, dst):
        store = pltpu.make_async_copy(src, dst, out_sem.at[len(stores)])
        store.start()
        stores.append(store)

    def send(n, value):
        x_ref[...] = value
        at = slice(n * PART, (n + 1) * PART)
        to_wire(x_ref, wire_ref, n * PART)
        keep(wire_ref.at[:, at, :], wire_hbm.at[:, at, :])

    offset = state_index() * PART
    loads[0].wait()
    second = pick(tok_ref, emit_cols_ref)
    loads[1].wait()
    loads[2].wait()
    y = alpha_ref[...]
    sums = []
    for t in range(STEPS):
        x = dot(y, cols_ref[...])
        y32 = x * spread(step_of(second, t))
        sums.append(jnp.sum(y32, axis=1, keepdims=True))
        if t < STEPS - 1:
            y = y32.astype(BF16)
            y_ref[t] = y
        send(t, x)
    keep(y_ref, y_hbm)

    loads[3].wait()
    first = pick(tok_ref, emit_rows_ref)
    f0, f1 = (spread(step_of(first, t)) for t in range(2))
    loads[4].wait()
    for t in range(STEPS):
        column = column_of(step_of(second, t), offset)
        w = spread(step_of(first, t)) * column * back_ref[t].astype(F32)
        wt_ref[t * ROWS : (t + 1) * ROWS, :] = w.astype(BF16)
    wt_ref[STEPS * ROWS :, :] = first.astype(BF16)
    loads[5].wait()
    v = dot_nt(wt_ref[...], rows_ref[...])
    ends = [v[3 * ROWS : 3 * ROWS + 8]]
    g_ref[:ROWS] = (v[ROWS : 2 * ROWS] * f0).astype(BF16)
    g_ref[ROWS : 2 * ROWS] = (v[2 * ROWS : 3 * ROWS] * f1).astype(BF16)
    g_ref[2 * ROWS :] = (v[3 * ROWS + 8 :] * first[:16]).astype(BF16)
    send(STEPS, v[:ROWS])
    v = dot_nt(g_ref[...], rows_ref[...])
    ends.append(v[2 * ROWS : 2 * ROWS + 8])
    g_ref[:ROWS] = (v[ROWS : 2 * ROWS] * f0).astype(BF16)
    tail = (v[2 * ROWS + 8 :] * first[:8]).astype(BF16)
    g_ref[ROWS : ROWS + 16] = jnp.concatenate([tail, tail], axis=0)
    send(STEPS + 1, v[:ROWS])
    v = dot_nt(g_ref[: ROWS + 16], rows_ref[...])
    ends.append(v[ROWS : ROWS + 8])
    send(STEPS + 2, v[:ROWS])

    norm = jnp.zeros((1, 128), F32)
    for t in range(STEPS):
        part = sums[t] * column_of(ends[t], offset)
        at = STEPS * (iota((ROWS, 128), 0) >> 4) + t
        norm = norm + jnp.sum(jnp.where(iota((ROWS, 128), 1) == at, part, 0.0), axis=0, keepdims=True)
    high = norm.astype(BF16).astype(F32)
    middle = (norm - high).astype(BF16).astype(F32)
    low = norm - high - middle
    row = iota((8, 128), 0)
    parts = jnp.where(row == 0, high, jnp.where(row == 1, middle, jnp.where(row == 2, low, 0.0)))
    wire_ref[:, NORM:WIRE, :] = jnp.broadcast_to(parts.astype(BF16)[None], (PEERS, 8, 128))
    keep(wire_ref.at[:, NORM:WIRE, :], wire_hbm.at[:, NORM:WIRE, :])
    for store in stores:
        store.wait()


def to_row(column):
    return jnp.sum(
        jnp.where(iota((128, 128), 0) == iota((128, 128), 1), column, 0.0), axis=0, keepdims=True
    )


def local_kernel(
    tok_ref, rows_ref, cols_ref, emit_rows_ref, emit_cols_ref, back_ref,
    weight_ref, turned_ref, factor_ref, local_ref, take_rows_ref, take_cols_ref,
):
    me = state_index()
    first = pick(tok_ref, emit_rows_ref)
    second = pick(tok_ref, emit_cols_ref)
    pair = (iota((SEQ_DEV, ROWS), 1) >> 4 == iota((SEQ_DEV, ROWS), 0)).astype(F32).astype(BF16)
    for t in range(STEPS):
        column = column_of(step_of(second, t), me * PART)
        w = spread(step_of(first, t)) * column * back_ref[t].astype(F32)
        weight_ref[:, t * ROWS : (t + 1) * ROWS] = w.T.astype(BF16)
        factor_ref[t] = dot_tn(step_of(first, t).astype(BF16), pair).astype(BF16)
        if t == STEPS - 1:
            local_ref[...] = to_row(column)

    @pl.loop(0, WIDTH // 128)
    def _(b):
        at = pl.ds(pl.multiple_of(b * 128, 128), 128)
        turned_ref[at, :] = rows_ref[:, at].astype(F32).T.astype(BF16)

    mine = (lax.axis_index("dp") * PEERS + me) * 4
    hot = (iota((8, WIDTH), 1) == mine + iota((8, WIDTH), 0)) & (iota((8, WIDTH), 0) < 4)
    hot = hot.astype(F32).astype(BF16)
    take_rows_ref[...] = dot_nt(hot, rows_ref[...])
    take_cols_ref[...] = dot_nt(hot, cols_ref[...])


def counts_kernel(
    wire_ref, y_hbm, alpha_hbm, turned_hbm, factor_hbm, local_hbm, weight_hbm,
    out_hbm, keep_ref, give_ref, total_ref,
    y_ref, alpha_ref, turned_ref, factor_ref, local_ref, weight_ref, out_ref, ys_ref, m_ref,
    in_sem, out_sem,
):
    pairs = [
        (y_hbm, y_ref), (alpha_hbm, alpha_ref), (turned_hbm, turned_ref),
        (factor_hbm, factor_ref), (local_hbm, local_ref), (weight_hbm, weight_ref),
    ]
    loads = [pltpu.make_async_copy(a, b, in_sem.at[n]) for n, (a, b) in enumerate(pairs)]
    for load in loads:
        load.start()
    core = lax.axis_index("core")
    half = WIDTH // 2

    def put(term, side, rows, lanes, value):
        @pl.when(core == side)
        def _():
            keep_ref[term, rows, lanes] = value.astype(BF16)

        @pl.when(core != side)
        def _():
            give_ref[term, rows, lanes] = value.astype(BF16)

    totals = total_of(wire_ref)
    total_ref[...] = totals
    inverse = [inverse_norm(totals, t) for t in range(STEPS)]
    inv = [to_row(i) for i in inverse]

    def x_of(t):
        return wire_ref[:, t * PART : (t + 1) * PART, :].reshape(WIDTH, ROWS)

    m_ref[:, :ROWS] = (x_of(0).astype(F32) * inv[0]).astype(BF16)
    loads[0].wait()
    loads[1].wait()
    for t in range(STEPS):
        y = alpha_ref[...] if t == 0 else y_ref[t - 1]
        ys_ref[t * ROWS : (t + 1) * ROWS] = (y.astype(F32) * inverse[t]).astype(BF16)
    for b in range(4):
        peers = slice(b * 16, (b + 1) * 16)
        v = jnp.concatenate(
            [
                wire_ref[peers, (STEPS + t) * PART : (STEPS + t + 1) * PART, :].reshape(256, ROWS)
                for t in range(STEPS)
            ],
            axis=1,
        )
        value = dot(v, ys_ref[...])
        for side in range(2):
            part = value[:, side * half : (side + 1) * half]
            put(1, side, slice(b * 256, (b + 1) * 256), slice(0, half), part)

    loads[2].wait()
    loads[3].wait()
    loads[4].wait()
    f0, f1, f2 = (factor_ref[t].astype(F32) for t in range(STEPS))
    h = dot(turned_ref[...], jnp.concatenate([x_of(1), x_of(2)], axis=1))
    m_ref[:, ROWS : 2 * ROWS] = (h[:, :ROWS] * f0 * inv[1]).astype(BF16)
    h = dot(turned_ref[...], (h[:, ROWS:] * f0).astype(BF16)) * f1
    m_ref[:, 2 * ROWS :] = (h * inv[2]).astype(BF16)
    a = dot(turned_ref[...], h.astype(BF16)) * f2 * (local_ref[...] * inv[2])
    out_ref[...] = a.astype(BF16).reshape(PEERS, PART, ROWS)
    send = pltpu.make_async_copy(out_ref, out_hbm, out_sem)
    send.start()
    loads[5].wait()
    for b in range(4):
        value = dot_nt(weight_ref[...], m_ref[b * 256 : (b + 1) * 256, :])
        put(0, b // 2, slice(0, WIDTH), slice((b & 1) * 256, (b & 1) * 256 + 256), value)
    send.wait()


def place(turn):
    x, y = lax.axis_index("dp"), lax.axis_index("y")
    return jnp.where((lax.axis_index("core") == 0) != turn, x, y)


def pair_kernel(keep_ref, got_ref, own_hbm, *refs):
    outs, own_ref, sem = [refs[3], *refs[:3]], refs[3], refs[4]
    along_dp = lax.axis_index("core") == 0
    me = place(False)
    for d in (2, 1, 3, 0):
        to = (me + d) & 3
        for b in range(4):
            row = jnp.where(along_dp, to * 256 + b * 64, b * 256 + to * 64)
            at = pl.ds(pl.multiple_of(row, 64), 64)
            for term in range(2):
                total = keep_ref[term, at, :].astype(F32) + got_ref[term, at, :].astype(F32)
                outs[d][term, b * 64 : (b + 1) * 64, :] = total.astype(BF16)
    own = pltpu.make_async_copy(own_ref, own_hbm, sem)
    own.start()
    own.wait()


def plane_kernel(own_hbm, *refs):
    others, outs, (sum_ref, own_ref, sem) = refs[:3], refs[3:7], refs[7:]
    own = pltpu.make_async_copy(own_hbm, own_ref, sem)
    own.start()
    me = place(True)
    sum_ref[...] = sum(r[...].astype(F32) for r in others)
    own.wait()
    sum_ref[...] += own_ref[...].astype(F32)
    for d in range(4):
        at = pl.ds(pl.multiple_of(((me + d) & 3) * 64, 64), 64)
        outs[d][...] = sum_ref[:, at, :].astype(BF16)


def line_kernel(*refs):
    ins, out_ref = refs[:4], refs[4]
    for term in range(2):
        total = sum(r[term].astype(F32) for r in ins)
        for z in range(8):
            out_ref[z, term * 8 : (term + 1) * 8, :] = total[z * 8 : (z + 1) * 8, :].astype(BF16)


def final_kernel(wire_ref, out_ref):
    def store(s, lanes, tile):
        out_ref[s * PART : (s + 1) * PART, lanes] = tile.astype(BF16)

    from_wire(wire_ref, 0, store)


def call(kernel, name, outs, scratch=(), flops=10**9, moved=8 * 10**6, limit=VMEM, specs=None):
    return pl.pallas_call(
        kernel,
        name=name,
        out_shape=[jax.ShapeDtypeStruct(s, d) for s, d in outs],
        scratch_shapes=[s if hasattr(s, "dtype") else pltpu.VMEM(*s) for s in scratch],
        compiler_params=pltpu.CompilerParams(vmem_limit_bytes=limit),
        cost_estimate=pl.CostEstimate(flops=flops, bytes_accessed=moved, transcendentals=0),
        **(specs or {}),
    )


def ring(x, d, turn):
    pairs = []
    for a in range(4):
        for b in range(4):
            for c in range(2):
                over_dp = (c == 0) != turn
                to = ((a + d) % 4, b) if over_dp else (a, (b + d) % 4)
                pairs.append(((a * 4 + b) * 2 + c, (to[0] * 4 + to[1]) * 2 + c))
    return lax.ppermute(x, ("dp", "y", "core"), pairs)


def in_hbm(*arrays):
    return [pltpu.with_memory_space_constraint(v, pltpu.HBM) for v in arrays]


def on_device(alpha_init, tokens, trans_rows, trans_cols, emit_rows, emit_cols, backward):
    alpha = alpha_init.reshape(ROWS, WIDTH)
    back = jnp.swapaxes(backward, 2, 3).reshape(STEPS, ROWS, WIDTH)
    tok = tokens.T
    half = WIDTH // 2
    state = ("y", "z", "core")

    hbm = pl.BlockSpec(memory_space=pltpu.HBM)
    wire_shape, y_shape = (PEERS, WIRE, ROWS), (STEPS - 1, ROWS, WIDTH)
    square, emit_shape = (WIDTH, WIDTH), emit_rows.shape
    wire, y = call(
        send_kernel, "send", [(wire_shape, BF16), (y_shape, BF16)],
        [
            ((ROWS, WIDTH), BF16), (square, BF16), (square, BF16), (emit_shape, BF16),
            (emit_shape, BF16), ((STEPS, ROWS, WIDTH), BF16), (wire_shape, BF16),
            (y_shape, BF16), ((ROWS, WIDTH), F32), ((STEPS * (ROWS + 8), WIDTH), BF16),
            ((2 * (ROWS + 8), WIDTH), BF16), pltpu.SemaphoreType.DMA((6,)),
            pltpu.SemaphoreType.DMA((8,)),
        ],
        limit=ALONE,
        specs=dict(
            in_specs=[pl.BlockSpec(memory_space=pltpu.VMEM)] + [hbm] * 6, out_specs=[hbm] * 2
        ),
    )(tok, alpha, trans_rows, trans_cols, emit_rows, emit_cols, back)
    got = lax.all_to_all(wire, state, 0, 0, tiled=True)

    weight, turned, factor, local, take_rows, take_cols = call(
        local_kernel, "local",
        [
            ((WIDTH, STEPS * ROWS), BF16), (square, BF16), ((STEPS, WIDTH, ROWS), BF16),
            ((1, ROWS), F32), ((8, WIDTH), F32), ((8, WIDTH), F32),
        ],
        limit=ALONE,
    )(tok, trans_rows, trans_cols, emit_rows, emit_cols, back)

    a_shape = (PEERS, PART, ROWS)
    vmem = pl.BlockSpec(memory_space=pltpu.VMEM)
    a_wire, keep, give, total = call(
        counts_kernel, "counts",
        [(a_shape, BF16), ((2, WIDTH, half), BF16), ((2, WIDTH, half), BF16), ((1, 128), F32)],
        [
            (y_shape, BF16), ((ROWS, WIDTH), BF16), (square, BF16),
            ((STEPS, WIDTH, ROWS), BF16), ((1, ROWS), F32), ((WIDTH, STEPS * ROWS), BF16),
            (a_shape, BF16), ((STEPS * ROWS, WIDTH), BF16), ((WIDTH, STEPS * ROWS), BF16),
            pltpu.SemaphoreType.DMA((6,)), pltpu.SemaphoreType.DMA(()),
        ],
        limit=40 * 2**20,
        specs=dict(in_specs=[vmem] + [hbm] * 6, out_specs=[hbm] + [vmem] * 3),
    )(got, *in_hbm(y, alpha, turned, factor, local, weight))
    core = lax.axis_index("core")
    swap_cores = [(0, 1), (1, 0)]
    shape, small = (2, 256, half), (2, 64, half)
    own, *pieces = call(
        pair_kernel, "pair", [(shape, BF16)] * 4, [(shape, BF16), pltpu.SemaphoreType.DMA(())],
        specs=dict(out_specs=[hbm] + [vmem] * 3),
    )(keep, lax.ppermute(give, "core", swap_cores))
    far, right, left = (ring(pieces[d - 1], d, False) for d in (2, 1, 3))
    mark, *_ = lax.optimization_barrier((total, *pieces))
    a_wire, _ = lax.optimization_barrier((a_wire, lax.ppermute(mark, "core", swap_cores)))
    a_got = lax.all_to_all(a_wire, state, 0, 0, tiled=True)
    own, *pieces = call(
        plane_kernel, "plane", [(small, BF16)] * 4,
        [(shape, F32), (shape, BF16), pltpu.SemaphoreType.DMA(())],
        specs=dict(in_specs=[hbm] + [vmem] * 3),
    )(*in_hbm(own), far, right, left)
    far, right, left = (ring(pieces[d - 1], d, True) for d in (2, 1, 3))
    (part,) = call(line_kernel, "line", [((8, 16, half), BF16)])(own, far, right, left)
    (alpha_final,) = call(final_kernel, "final", [((ROWS, WIDTH), BF16)])(a_got)
    part = lax.all_to_all(part, "z", 0, 0, tiled=True)
    loglik = jnp.log(total[0, 2 : 3 * SEQ_DEV : 3] / (WIDTH * WIDTH))
    part, alpha_final, loglik = lax.optimization_barrier((part, alpha_final, loglik))
    part = jnp.sum(part.astype(F32), axis=0)
    part = part.reshape(2, 2, 4, half)
    mine = jnp.where(core == 0, part[:, 0], part[:, 1])
    other = lax.ppermute(jnp.where(core == 0, part[:, 1], part[:, 0]), "core", swap_cores)
    left, right = jnp.where(core == 0, mine, other), jnp.where(core == 0, other, mine)
    sums = jnp.concatenate([left, right], axis=2)
    scale = 1.0 / (SEQ_DEV * 4 * STEPS)
    counts_rows = sums[0] * take_rows[:4] * scale
    counts_cols = sums[1] * take_cols[:4] * scale

    return (
        alpha_final.reshape(SEQ_DEV, PART, WIDTH),
        counts_rows.T,
        counts_cols.T,
        loglik,
    )


def solution(mesh):
    mesh = jax.sharding.Mesh(mesh.devices.reshape(4, 4, 8, 2), ("dp", "y", "z", "core"))
    state = ("y", "z", "core")
    return jax.shard_map(
        on_device,
        mesh=mesh,
        in_specs=(
            P("dp", state, None),
            P("dp", None),
            P(),
            P(),
            P(),
            P(),
            P(None, "dp", None, state),
        ),
        out_specs=(
            P("dp", state, None),
            P(None, ("dp", *state)),
            P(None, ("dp", *state)),
            P("dp"),
        ),
        check_vma=False,
    )
```

```python
import jax
import jax.numpy as jnp
from jax import lax
from jax.experimental import pallas as pl
from jax.experimental.pallas import tpu as pltpu
from jax.sharding import PartitionSpec as P

STEPS = 3
F32 = jnp.float32
BF16 = jnp.bfloat16
SEQ_DEV = 8
PART = 16
ROWS = SEQ_DEV * PART
WIDTH = 1024
PEERS = WIDTH // PART
VMEM = 24 * 2**20
ALONE = 60 * 2**20
NORM = 2 * STEPS * PART
WIRE = NORM + 8


def iota(shape, dim):
    return lax.broadcasted_iota(jnp.int32, shape, dim)


def dot(a, b):
    return lax.dot_general(a, b, (((1,), (0,)), ((), ())), preferred_element_type=F32)


def dot_nt(a, b):
    return lax.dot_general(a, b, (((1,), (1,)), ((), ())), preferred_element_type=F32)


def dot_tn(a, b):
    return lax.dot_general(a, b, (((0,), (0,)), ((), ())), preferred_element_type=F32)


def pick(tok_ref, emit_ref):
    rows = emit_ref.shape[0]
    hot = [
        (tok_ref[t : t + 1, :] == iota((rows, SEQ_DEV), 0)).astype(F32) for t in range(STEPS)
    ]
    return dot_tn(jnp.concatenate(hot, axis=1).astype(BF16), emit_ref[...])


def step_of(v, t):
    return v[t * SEQ_DEV : (t + 1) * SEQ_DEV]


def spread(v):
    n = v.shape[-1]
    return jnp.broadcast_to(v[:, None, :], (SEQ_DEV, PART, n)).reshape(ROWS, n)


def column_of(v, offset):
    at = offset + (iota((ROWS, WIDTH), 0) & (PART - 1))
    return jnp.sum(jnp.where(iota((ROWS, WIDTH), 1) == at, spread(v), 0.0), axis=1, keepdims=True)


def swap(tiles):
    group = iota((PART, 128), 1) >> 4
    for bit in (1, 2, 4):
        low = (group & bit) == 0
        out = list(tiles)
        for s in range(SEQ_DEV):
            if s & bit == 0:
                a, b = tiles[s], tiles[s + bit]
                out[s] = jnp.where(low, a, pltpu.roll(b, PART * bit, 1))
                out[s + bit] = jnp.where(low, pltpu.roll(a, 128 - PART * bit, 1), b)
        tiles = out
    return tiles


def to_wire(src_ref, dst_ref, row):
    for g in range(PEERS // SEQ_DEV):
        lanes = slice(g * 128, (g + 1) * 128)
        tiles = swap([src_ref[s * PART : (s + 1) * PART, lanes] for s in range(SEQ_DEV)])
        for s in range(SEQ_DEV):
            dst_ref[g * SEQ_DEV + s, row : row + PART, :] = tiles[s].astype(BF16)


def from_wire(src_ref, row, store):
    for g in range(PEERS // SEQ_DEV):
        tiles = swap(
            [src_ref[g * SEQ_DEV + s, row : row + PART, :].astype(F32) for s in range(SEQ_DEV)]
        )
        lanes = slice(g * 128, (g + 1) * 128)
        for s in range(SEQ_DEV):
            store(s, lanes, tiles[s])


def state_index():
    return (lax.axis_index("y") * 8 + lax.axis_index("z")) * 2 + lax.axis_index("core")


def total_of(wire_ref):
    return jnp.sum(jnp.sum(wire_ref[:, NORM:WIRE, :].astype(F32), axis=0), axis=0, keepdims=True)


def inverse_norm(totals, t):
    at = STEPS * (iota((ROWS, 128), 0) >> 4) + t
    total = jnp.sum(jnp.where(iota((ROWS, 128), 1) == at, totals, 0.0), axis=1, keepdims=True)
    return float(WIDTH * WIDTH) / total


def send_kernel(
    tok_ref, alpha_hbm, rows_hbm, cols_hbm, emit_rows_hbm, emit_cols_hbm, back_hbm,
    wire_hbm, y_hbm, alpha_ref, rows_ref, cols_ref, emit_rows_ref, emit_cols_ref, back_ref,
    wire_ref, y_ref, x_ref, wt_ref, g_ref, in_sem, out_sem,
):
    pairs = [
        (emit_cols_hbm, emit_cols_ref), (alpha_hbm, alpha_ref), (cols_hbm, cols_ref),
        (emit_rows_hbm, emit_rows_ref), (back_hbm, back_ref), (rows_hbm, rows_ref),
    ]
    loads = [pltpu.make_async_copy(a, b, in_sem.at[n]) for n, (a, b) in enumerate(pairs)]
    for load in loads:
        load.start()
    stores = []

    def keep(src, dst):
        store = pltpu.make_async_copy(src, dst, out_sem.at[len(stores)])
        store.start()
        stores.append(store)

    def send(n, value):
        x_ref[...] = value
        at = slice(n * PART, (n + 1) * PART)
        to_wire(x_ref, wire_ref, n * PART)
        keep(wire_ref.at[:, at, :], wire_hbm.at[:, at, :])

    offset = state_index() * PART
    loads[0].wait()
    second = pick(tok_ref, emit_cols_ref)
    loads[1].wait()
    loads[2].wait()
    y = alpha_ref[...]
    sums = []
    for t in range(STEPS):
        x = dot(y, cols_ref[...])
        y32 = x * spread(step_of(second, t))
        sums.append(jnp.sum(y32, axis=1, keepdims=True))
        if t < STEPS - 1:
            y = y32.astype(BF16)
            y_ref[t] = y
        send(t, x)
    keep(y_ref, y_hbm)

    loads[3].wait()
    first = pick(tok_ref, emit_rows_ref)
    f0, f1 = (spread(step_of(first, t)) for t in range(2))
    loads[4].wait()
    for t in range(STEPS):
        column = column_of(step_of(second, t), offset)
        w = spread(step_of(first, t)) * column * back_ref[t].astype(F32)
        wt_ref[t * ROWS : (t + 1) * ROWS, :] = w.astype(BF16)
    wt_ref[STEPS * ROWS :, :] = first.astype(BF16)
    loads[5].wait()
    v = dot_nt(wt_ref[...], rows_ref[...])
    ends = [v[3 * ROWS : 3 * ROWS + 8]]
    g_ref[:ROWS] = (v[ROWS : 2 * ROWS] * f0).astype(BF16)
    g_ref[ROWS : 2 * ROWS] = (v[2 * ROWS : 3 * ROWS] * f1).astype(BF16)
    g_ref[2 * ROWS :] = (v[3 * ROWS + 8 :] * first[:16]).astype(BF16)
    send(STEPS, v[:ROWS])
    v = dot_nt(g_ref[...], rows_ref[...])
    ends.append(v[2 * ROWS : 2 * ROWS + 8])
    g_ref[:ROWS] = (v[ROWS : 2 * ROWS] * f0).astype(BF16)
    tail = (v[2 * ROWS + 8 :] * first[:8]).astype(BF16)
    g_ref[ROWS : ROWS + 16] = jnp.concatenate([tail, tail], axis=0)
    send(STEPS + 1, v[:ROWS])
    v = dot_nt(g_ref[: ROWS + 16], rows_ref[...])
    ends.append(v[ROWS : ROWS + 8])
    send(STEPS + 2, v[:ROWS])

    norm = jnp.zeros((1, 128), F32)
    for t in range(STEPS):
        part = sums[t] * column_of(ends[t], offset)
        at = STEPS * (iota((ROWS, 128), 0) >> 4) + t
        norm = norm + jnp.sum(jnp.where(iota((ROWS, 128), 1) == at, part, 0.0), axis=0, keepdims=True)
    high = norm.astype(BF16).astype(F32)
    middle = (norm - high).astype(BF16).astype(F32)
    low = norm - high - middle
    row = iota((8, 128), 0)
    parts = jnp.where(row == 0, high, jnp.where(row == 1, middle, jnp.where(row == 2, low, 0.0)))
    wire_ref[:, NORM:WIRE, :] = jnp.broadcast_to(parts.astype(BF16)[None], (PEERS, 8, 128))
    keep(wire_ref.at[:, NORM:WIRE, :], wire_hbm.at[:, NORM:WIRE, :])
    for store in stores:
        store.wait()


def to_row(column):
    return jnp.sum(
        jnp.where(iota((128, 128), 0) == iota((128, 128), 1), column, 0.0), axis=0, keepdims=True
    )


def local_kernel(
    tok_ref, rows_ref, cols_ref, emit_rows_ref, emit_cols_ref, back_ref,
    weight_ref, turned_ref, factor_ref, local_ref, take_rows_ref, take_cols_ref,
):
    me = state_index()
    first = pick(tok_ref, emit_rows_ref)
    second = pick(tok_ref, emit_cols_ref)
    pair = (iota((SEQ_DEV, ROWS), 1) >> 4 == iota((SEQ_DEV, ROWS), 0)).astype(F32).astype(BF16)
    for t in range(STEPS):
        column = column_of(step_of(second, t), me * PART)
        w = spread(step_of(first, t)) * column * back_ref[t].astype(F32)
        weight_ref[:, t * ROWS : (t + 1) * ROWS] = w.T.astype(BF16)
        factor_ref[t] = dot_tn(step_of(first, t).astype(BF16), pair).astype(BF16)
        if t == STEPS - 1:
            local_ref[...] = to_row(column)

    @pl.loop(0, WIDTH // 128)
    def _(b):
        at = pl.ds(pl.multiple_of(b * 128, 128), 128)
        turned_ref[at, :] = rows_ref[:, at].astype(F32).T.astype(BF16)

    mine = (lax.axis_index("dp") * PEERS + me) * 4
    hot = (iota((8, WIDTH), 1) == mine + iota((8, WIDTH), 0)) & (iota((8, WIDTH), 0) < 4)
    hot = hot.astype(F32).astype(BF16)
    take_rows_ref[...] = dot_nt(hot, rows_ref[...])
    take_cols_ref[...] = dot_nt(hot, cols_ref[...])


def counts_kernel(
    wire_ref, y_hbm, alpha_hbm, turned_hbm, factor_hbm, weight_hbm,
    after_ref, keep_ref, give_ref, total_ref,
    y_ref, alpha_ref, turned_ref, factor_ref, weight_ref, ys_ref, m_ref, in_sem,
):
    pairs = [
        (y_hbm, y_ref), (alpha_hbm, alpha_ref), (turned_hbm, turned_ref),
        (factor_hbm, factor_ref), (weight_hbm, weight_ref),
    ]
    loads = [pltpu.make_async_copy(a, b, in_sem.at[n]) for n, (a, b) in enumerate(pairs)]
    for load in loads:
        load.start()
    core = lax.axis_index("core")
    half = WIDTH // 2

    targets = [
        (ref, pl.multiple_of(side * half, half))
        for ref, side in ((keep_ref, core), (give_ref, 1 - core))
    ]

    totals = total_of(wire_ref)
    total_ref[...] = totals
    inverse = [inverse_norm(totals, t) for t in range(STEPS)]
    inv = [to_row(i) for i in inverse]

    def x_of(t):
        return wire_ref[:, t * PART : (t + 1) * PART, :].reshape(WIDTH, ROWS)

    m_ref[:, :ROWS] = (x_of(0).astype(F32) * inv[0]).astype(BF16)
    loads[0].wait()
    loads[1].wait()
    for t in range(STEPS):
        y = alpha_ref[...] if t == 0 else y_ref[t - 1]
        ys_ref[t * ROWS : (t + 1) * ROWS] = (y.astype(F32) * inverse[t]).astype(BF16)
    for b in range(4):
        peers = slice(b * 16, (b + 1) * 16)
        v = jnp.concatenate(
            [
                wire_ref[peers, (STEPS + t) * PART : (STEPS + t + 1) * PART, :].reshape(256, ROWS)
                for t in range(STEPS)
            ],
            axis=1,
        )
        for ref, start in targets:
            ref[1, b * 256 : (b + 1) * 256, :] = dot(v, ys_ref[:, pl.ds(start, half)]).astype(BF16)

    loads[2].wait()
    loads[3].wait()
    f0, f1 = (factor_ref[t].astype(F32) for t in range(2))
    h = dot(turned_ref[...], jnp.concatenate([x_of(1), x_of(2)], axis=1))
    m_ref[:, ROWS : 2 * ROWS] = (h[:, :ROWS] * f0 * inv[1]).astype(BF16)
    h = dot(turned_ref[...], (h[:, ROWS:] * f0).astype(BF16)) * f1
    m_ref[:, 2 * ROWS :] = (h * inv[2]).astype(BF16)
    after_ref[...] = h.astype(BF16)
    loads[4].wait()
    for b in range(2):
        for ref, start in targets:
            at = pl.ds(pl.multiple_of(start + b * 256, 256), 256)
            value = dot_nt(weight_ref[...], m_ref[at, :])
            ref[0, :, b * 256 : (b + 1) * 256] = value.astype(BF16)


def alpha_kernel(after_ref, turned_ref, factor_ref, local_ref, total_ref, out_ref):
    inv = to_row(inverse_norm(total_ref[...], STEPS - 1))
    factor = factor_ref[STEPS - 1].astype(F32) * (local_ref[...] * inv)
    a = dot(turned_ref[...], after_ref[...]) * factor
    out_ref[...] = a.astype(BF16).reshape(PEERS, PART, ROWS)


def place(turn):
    x, y = lax.axis_index("dp"), lax.axis_index("y")
    return jnp.where((lax.axis_index("core") == 0) != turn, x, y)


def pair_kernel(keep_ref, got_ref, own_hbm, *refs):
    outs, own_ref, sem = [refs[3], *refs[:3]], refs[3], refs[4]
    along_dp = lax.axis_index("core") == 0
    me = place(False)
    for d in (2, 1, 3, 0):
        to = (me + d) & 3
        for b in range(4):
            row = jnp.where(along_dp, to * 256 + b * 64, b * 256 + to * 64)
            at = pl.ds(pl.multiple_of(row, 64), 64)
            for term in range(2):
                total = keep_ref[term, at, :].astype(F32) + got_ref[term, at, :].astype(F32)
                outs[d][term, b * 64 : (b + 1) * 64, :] = total.astype(BF16)
    own = pltpu.make_async_copy(own_ref, own_hbm, sem)
    own.start()
    own.wait()


def plane_kernel(own_hbm, *refs):
    others, outs, (sum_ref, own_ref, sem) = refs[:3], refs[3:7], refs[7:]
    own = pltpu.make_async_copy(own_hbm, own_ref, sem)
    own.start()
    me = place(True)
    sum_ref[...] = sum(r[...].astype(F32) for r in others)
    own.wait()
    sum_ref[...] += own_ref[...].astype(F32)
    for d in range(4):
        at = pl.ds(pl.multiple_of(((me + d) & 3) * 64, 64), 64)
        outs[d][...] = sum_ref[:, at, :].astype(BF16)


def line_kernel(*refs):
    ins, out_ref = refs[:4], refs[4]
    for term in range(2):
        total = sum(r[term].astype(F32) for r in ins)
        for z in range(8):
            out_ref[z, term * 8 : (term + 1) * 8, :] = total[z * 8 : (z + 1) * 8, :].astype(BF16)


def final_kernel(wire_ref, out_ref):
    def store(s, lanes, tile):
        out_ref[s * PART : (s + 1) * PART, lanes] = tile.astype(BF16)

    from_wire(wire_ref, 0, store)


def call(kernel, name, outs, scratch=(), flops=10**9, moved=8 * 10**6, limit=VMEM, specs=None):
    return pl.pallas_call(
        kernel,
        name=name,
        out_shape=[jax.ShapeDtypeStruct(s, d) for s, d in outs],
        scratch_shapes=[s if hasattr(s, "dtype") else pltpu.VMEM(*s) for s in scratch],
        compiler_params=pltpu.CompilerParams(vmem_limit_bytes=limit),
        cost_estimate=pl.CostEstimate(flops=flops, bytes_accessed=moved, transcendentals=0),
        **(specs or {}),
    )


def ring(x, d, turn):
    pairs = []
    for a in range(4):
        for b in range(4):
            for c in range(2):
                over_dp = (c == 0) != turn
                to = ((a + d) % 4, b) if over_dp else (a, (b + d) % 4)
                pairs.append(((a * 4 + b) * 2 + c, (to[0] * 4 + to[1]) * 2 + c))
    return lax.ppermute(x, ("dp", "y", "core"), pairs)


def in_hbm(*arrays):
    return [pltpu.with_memory_space_constraint(v, pltpu.HBM) for v in arrays]


def on_device(alpha_init, tokens, trans_rows, trans_cols, emit_rows, emit_cols, backward):
    alpha = alpha_init.reshape(ROWS, WIDTH)
    back = jnp.swapaxes(backward, 2, 3).reshape(STEPS, ROWS, WIDTH)
    tok = tokens.T
    half = WIDTH // 2
    state = ("y", "z", "core")

    hbm = pl.BlockSpec(memory_space=pltpu.HBM)
    wire_shape, y_shape = (PEERS, WIRE, ROWS), (STEPS - 1, ROWS, WIDTH)
    square, emit_shape = (WIDTH, WIDTH), emit_rows.shape
    wire, y = call(
        send_kernel, "send", [(wire_shape, BF16), (y_shape, BF16)],
        [
            ((ROWS, WIDTH), BF16), (square, BF16), (square, BF16), (emit_shape, BF16),
            (emit_shape, BF16), ((STEPS, ROWS, WIDTH), BF16), (wire_shape, BF16),
            (y_shape, BF16), ((ROWS, WIDTH), F32), ((STEPS * (ROWS + 8), WIDTH), BF16),
            ((2 * (ROWS + 8), WIDTH), BF16), pltpu.SemaphoreType.DMA((6,)),
            pltpu.SemaphoreType.DMA((8,)),
        ],
        limit=ALONE,
        specs=dict(
            in_specs=[pl.BlockSpec(memory_space=pltpu.VMEM)] + [hbm] * 6, out_specs=[hbm] * 2
        ),
    )(tok, alpha, trans_rows, trans_cols, emit_rows, emit_cols, back)
    got = lax.all_to_all(wire, state, 0, 0, tiled=True)

    weight, turned, factor, local, take_rows, take_cols = call(
        local_kernel, "local",
        [
            ((WIDTH, STEPS * ROWS), BF16), (square, BF16), ((STEPS, WIDTH, ROWS), BF16),
            ((1, ROWS), F32), ((8, WIDTH), F32), ((8, WIDTH), F32),
        ],
        limit=ALONE,
    )(tok, trans_rows, trans_cols, emit_rows, emit_cols, back)

    a_shape = (PEERS, PART, ROWS)
    vmem = pl.BlockSpec(memory_space=pltpu.VMEM)
    after, keep, give, total = call(
        counts_kernel, "counts",
        [
            ((WIDTH, ROWS), BF16), ((2, WIDTH, half), BF16), ((2, WIDTH, half), BF16),
            ((1, 128), F32),
        ],
        [
            (y_shape, BF16), ((ROWS, WIDTH), BF16), (square, BF16),
            ((STEPS, WIDTH, ROWS), BF16), ((WIDTH, STEPS * ROWS), BF16),
            ((STEPS * ROWS, WIDTH), BF16), ((WIDTH, STEPS * ROWS), BF16),
            pltpu.SemaphoreType.DMA((5,)),
        ],
        limit=40 * 2**20,
        specs=dict(in_specs=[vmem] + [hbm] * 5, out_specs=[vmem] * 4),
    )(got, *in_hbm(y, alpha, turned, factor, weight))
    (a_wire,) = call(alpha_kernel, "alpha", [(a_shape, BF16)])(
        after, *in_hbm(turned, factor, local), total
    )

    keep, a_wire = lax.optimization_barrier((keep, a_wire))

    core = lax.axis_index("core")
    swap_cores = [(0, 1), (1, 0)]
    shape, small = (2, 256, half), (2, 64, half)
    own, *pieces = call(
        pair_kernel, "pair", [(shape, BF16)] * 4, [(shape, BF16), pltpu.SemaphoreType.DMA(())],
        specs=dict(out_specs=[hbm] + [vmem] * 3),
    )(keep, lax.ppermute(give, "core", swap_cores))
    far, right, left = (ring(pieces[d - 1], d, False) for d in (2, 1, 3))
    mark, *_ = lax.optimization_barrier((total, *pieces))
    a_wire, _ = lax.optimization_barrier((a_wire, lax.ppermute(mark, "core", swap_cores)))
    a_got = lax.all_to_all(a_wire, state, 0, 0, tiled=True)
    own, *pieces = call(
        plane_kernel, "plane", [(small, BF16)] * 4,
        [(shape, F32), (shape, BF16), pltpu.SemaphoreType.DMA(())],
        specs=dict(in_specs=[hbm] + [vmem] * 3),
    )(*in_hbm(own), far, right, left)
    far, right, left = (ring(pieces[d - 1], d, True) for d in (2, 1, 3))
    (part,) = call(line_kernel, "line", [((8, 16, half), BF16)])(own, far, right, left)
    (alpha_final,) = call(final_kernel, "final", [((ROWS, WIDTH), BF16)])(a_got)
    part = lax.all_to_all(part, "z", 0, 0, tiled=True)
    loglik = jnp.log(total[0, 2 : 3 * SEQ_DEV : 3] / (WIDTH * WIDTH))
    part, alpha_final, loglik = lax.optimization_barrier((part, alpha_final, loglik))
    part = jnp.sum(part.astype(F32), axis=0)
    part = part.reshape(2, 2, 4, half)
    mine = jnp.where(core == 0, part[:, 0], part[:, 1])
    other = lax.ppermute(jnp.where(core == 0, part[:, 1], part[:, 0]), "core", swap_cores)
    left, right = jnp.where(core == 0, mine, other), jnp.where(core == 0, other, mine)
    sums = jnp.concatenate([left, right], axis=2)
    scale = 1.0 / (SEQ_DEV * 4 * STEPS)
    counts_rows = sums[0] * take_rows[:4] * scale
    counts_cols = sums[1] * take_cols[:4] * scale

    return (
        alpha_final.reshape(SEQ_DEV, PART, WIDTH),
        counts_rows.T,
        counts_cols.T,
        loglik,
    )


def solution(mesh):
    mesh = jax.sharding.Mesh(mesh.devices.reshape(4, 4, 8, 2), ("dp", "y", "z", "core"))
    state = ("y", "z", "core")
    return jax.shard_map(
        on_device,
        mesh=mesh,
        in_specs=(
            P("dp", state, None),
            P("dp", None),
            P(),
            P(),
            P(),
            P(),
            P(None, "dp", None, state),
        ),
        out_specs=(
            P("dp", state, None),
            P(None, ("dp", *state)),
            P(None, ("dp", *state)),
            P("dp"),
        ),
        check_vma=False,
    )
```

```python
import jax
import jax.numpy as jnp
from jax import lax
from jax.experimental import pallas as pl
from jax.experimental.pallas import tpu as pltpu
from jax.sharding import PartitionSpec as P

STEPS = 3
F32 = jnp.float32
BF16 = jnp.bfloat16
SEQ_DEV = 8
PART = 16
ROWS = SEQ_DEV * PART
WIDTH = 1024
PEERS = WIDTH // PART
VMEM = 24 * 2**20
ALONE = 60 * 2**20
NORM = 2 * STEPS * PART
WIRE = NORM + 8


def iota(shape, dim):
    return lax.broadcasted_iota(jnp.int32, shape, dim)


def dot(a, b):
    return lax.dot_general(a, b, (((1,), (0,)), ((), ())), preferred_element_type=F32)


def dot_nt(a, b):
    return lax.dot_general(a, b, (((1,), (1,)), ((), ())), preferred_element_type=F32)


def dot_tn(a, b):
    return lax.dot_general(a, b, (((0,), (0,)), ((), ())), preferred_element_type=F32)


def pick(tok_ref, emit_ref):
    rows = emit_ref.shape[0]
    hot = [
        (tok_ref[t : t + 1, :] == iota((rows, SEQ_DEV), 0)).astype(F32) for t in range(STEPS)
    ]
    return dot_tn(jnp.concatenate(hot, axis=1).astype(BF16), emit_ref[...])


def step_of(v, t):
    return v[t * SEQ_DEV : (t + 1) * SEQ_DEV]


def spread(v):
    n = v.shape[-1]
    return jnp.broadcast_to(v[:, None, :], (SEQ_DEV, PART, n)).reshape(ROWS, n)


def column_of(v, offset):
    at = offset + (iota((ROWS, WIDTH), 0) & (PART - 1))
    return jnp.sum(jnp.where(iota((ROWS, WIDTH), 1) == at, spread(v), 0.0), axis=1, keepdims=True)


def swap(tiles):
    group = iota((PART, 128), 1) >> 4
    for bit in (1, 2, 4):
        low = (group & bit) == 0
        out = list(tiles)
        for s in range(SEQ_DEV):
            if s & bit == 0:
                a, b = tiles[s], tiles[s + bit]
                out[s] = jnp.where(low, a, pltpu.roll(b, PART * bit, 1))
                out[s + bit] = jnp.where(low, pltpu.roll(a, 128 - PART * bit, 1), b)
        tiles = out
    return tiles


def to_wire(src_ref, dst_ref, row):
    for g in range(PEERS // SEQ_DEV):
        lanes = slice(g * 128, (g + 1) * 128)
        tiles = swap([src_ref[s * PART : (s + 1) * PART, lanes] for s in range(SEQ_DEV)])
        for s in range(SEQ_DEV):
            dst_ref[g * SEQ_DEV + s, row : row + PART, :] = tiles[s].astype(BF16)


def from_wire(src_ref, row, store):
    for g in range(PEERS // SEQ_DEV):
        tiles = swap(
            [src_ref[g * SEQ_DEV + s, row : row + PART, :].astype(F32) for s in range(SEQ_DEV)]
        )
        lanes = slice(g * 128, (g + 1) * 128)
        for s in range(SEQ_DEV):
            store(s, lanes, tiles[s])


def state_index():
    return (lax.axis_index("y") * 8 + lax.axis_index("z")) * 2 + lax.axis_index("core")


def total_of(wire_ref):
    return jnp.sum(jnp.sum(wire_ref[:, NORM:WIRE, :].astype(F32), axis=0), axis=0, keepdims=True)


def inverse_norm(totals, t):
    at = STEPS * (iota((ROWS, 128), 0) >> 4) + t
    total = jnp.sum(jnp.where(iota((ROWS, 128), 1) == at, totals, 0.0), axis=1, keepdims=True)
    return float(WIDTH * WIDTH) / total


def send_kernel(
    tok_ref, alpha_hbm, rows_hbm, cols_hbm, emit_rows_hbm, emit_cols_hbm, back_hbm,
    wire_hbm, y_hbm, alpha_ref, rows_ref, cols_ref, emit_rows_ref, emit_cols_ref, back_ref,
    wire_ref, y_ref, x_ref, wt_ref, g_ref, in_sem, out_sem,
):
    pairs = [
        (emit_cols_hbm, emit_cols_ref), (alpha_hbm, alpha_ref), (cols_hbm, cols_ref),
        (emit_rows_hbm, emit_rows_ref), (back_hbm, back_ref), (rows_hbm, rows_ref),
    ]
    loads = [pltpu.make_async_copy(a, b, in_sem.at[n]) for n, (a, b) in enumerate(pairs)]
    for load in loads:
        load.start()
    stores = []

    def keep(src, dst):
        store = pltpu.make_async_copy(src, dst, out_sem.at[len(stores)])
        store.start()
        stores.append(store)

    def send(n, value):
        x_ref[...] = value
        at = slice(n * PART, (n + 1) * PART)
        to_wire(x_ref, wire_ref, n * PART)
        keep(wire_ref.at[:, at, :], wire_hbm.at[:, at, :])

    offset = state_index() * PART
    loads[0].wait()
    second = pick(tok_ref, emit_cols_ref)
    loads[1].wait()
    loads[2].wait()
    y = alpha_ref[...]
    sums = []
    for t in range(STEPS):
        x = dot(y, cols_ref[...])
        y32 = x * spread(step_of(second, t))
        sums.append(jnp.sum(y32, axis=1, keepdims=True))
        if t < STEPS - 1:
            y = y32.astype(BF16)
            y_ref[t] = y
        send(t, x)
    keep(y_ref, y_hbm)

    loads[3].wait()
    first = pick(tok_ref, emit_rows_ref)
    f0, f1 = (spread(step_of(first, t)) for t in range(2))
    loads[4].wait()
    for t in range(STEPS):
        column = column_of(step_of(second, t), offset)
        w = spread(step_of(first, t)) * column * back_ref[t].astype(F32)
        wt_ref[t * ROWS : (t + 1) * ROWS, :] = w.astype(BF16)
    wt_ref[STEPS * ROWS :, :] = first.astype(BF16)
    loads[5].wait()
    v = dot_nt(wt_ref[...], rows_ref[...])
    ends = [v[3 * ROWS : 3 * ROWS + 8]]
    g_ref[:ROWS] = (v[ROWS : 2 * ROWS] * f0).astype(BF16)
    g_ref[ROWS : 2 * ROWS] = (v[2 * ROWS : 3 * ROWS] * f1).astype(BF16)
    g_ref[2 * ROWS :] = (v[3 * ROWS + 8 :] * first[:16]).astype(BF16)
    send(STEPS, v[:ROWS])
    v = dot_nt(g_ref[...], rows_ref[...])
    ends.append(v[2 * ROWS : 2 * ROWS + 8])
    g_ref[:ROWS] = (v[ROWS : 2 * ROWS] * f0).astype(BF16)
    tail = (v[2 * ROWS + 8 :] * first[:8]).astype(BF16)
    g_ref[ROWS : ROWS + 16] = jnp.concatenate([tail, tail], axis=0)
    send(STEPS + 1, v[:ROWS])
    v = dot_nt(g_ref[: ROWS + 16], rows_ref[...])
    ends.append(v[ROWS : ROWS + 8])
    send(STEPS + 2, v[:ROWS])

    norm = jnp.zeros((1, 128), F32)
    for t in range(STEPS):
        part = sums[t] * column_of(ends[t], offset)
        at = STEPS * (iota((ROWS, 128), 0) >> 4) + t
        norm = norm + jnp.sum(jnp.where(iota((ROWS, 128), 1) == at, part, 0.0), axis=0, keepdims=True)
    high = norm.astype(BF16).astype(F32)
    middle = (norm - high).astype(BF16).astype(F32)
    low = norm - high - middle
    row = iota((8, 128), 0)
    parts = jnp.where(row == 0, high, jnp.where(row == 1, middle, jnp.where(row == 2, low, 0.0)))
    wire_ref[:, NORM:WIRE, :] = jnp.broadcast_to(parts.astype(BF16)[None], (PEERS, 8, 128))
    keep(wire_ref.at[:, NORM:WIRE, :], wire_hbm.at[:, NORM:WIRE, :])
    for store in stores:
        store.wait()


def to_row(column):
    return jnp.sum(
        jnp.where(iota((128, 128), 0) == iota((128, 128), 1), column, 0.0), axis=0, keepdims=True
    )


def local_kernel(
    tok_ref, rows_ref, cols_ref, emit_rows_ref, emit_cols_ref, back_ref,
    weight_ref, turned_ref, factor_ref, local_ref, take_rows_ref, take_cols_ref,
):
    me = state_index()
    first = pick(tok_ref, emit_rows_ref)
    second = pick(tok_ref, emit_cols_ref)
    pair = (iota((SEQ_DEV, ROWS), 1) >> 4 == iota((SEQ_DEV, ROWS), 0)).astype(F32).astype(BF16)
    for t in range(STEPS):
        column = column_of(step_of(second, t), me * PART)
        w = spread(step_of(first, t)) * column * back_ref[t].astype(F32)
        weight_ref[:, t * ROWS : (t + 1) * ROWS] = w.T.astype(BF16)
        factor_ref[t] = dot_tn(step_of(first, t).astype(BF16), pair).astype(BF16)
        if t == STEPS - 1:
            local_ref[...] = to_row(column)

    @pl.loop(0, WIDTH // 128)
    def _(b):
        at = pl.ds(pl.multiple_of(b * 128, 128), 128)
        turned_ref[at, :] = rows_ref[:, at].astype(F32).T.astype(BF16)

    mine = (lax.axis_index("dp") * PEERS + me) * 4
    hot = (iota((8, WIDTH), 1) == mine + iota((8, WIDTH), 0)) & (iota((8, WIDTH), 0) < 4)
    hot = hot.astype(F32).astype(BF16)
    take_rows_ref[...] = dot_nt(hot, rows_ref[...])
    take_cols_ref[...] = dot_nt(hot, cols_ref[...])


def counts_kernel(
    wire_ref, y_hbm, alpha_hbm, turned_hbm, factor_hbm, weight_hbm,
    after_ref, keep_ref, give_ref, total_ref,
    y_ref, alpha_ref, turned_ref, factor_ref, weight_ref, ys_ref, m_ref, in_sem,
):
    pairs = [
        (y_hbm, y_ref), (alpha_hbm, alpha_ref), (turned_hbm, turned_ref),
        (factor_hbm, factor_ref), (weight_hbm, weight_ref),
    ]
    loads = [pltpu.make_async_copy(a, b, in_sem.at[n]) for n, (a, b) in enumerate(pairs)]
    for load in loads:
        load.start()
    core = lax.axis_index("core")
    half = WIDTH // 2

    targets = [
        (ref, pl.multiple_of(side * half, half))
        for ref, side in ((keep_ref, core), (give_ref, 1 - core))
    ]

    totals = total_of(wire_ref)
    total_ref[...] = totals
    inverse = [inverse_norm(totals, t) for t in range(STEPS)]
    inv = [to_row(i) for i in inverse]

    def x_of(t):
        return wire_ref[:, t * PART : (t + 1) * PART, :].reshape(WIDTH, ROWS)

    m_ref[:, :ROWS] = (x_of(0).astype(F32) * inv[0]).astype(BF16)
    loads[0].wait()
    loads[1].wait()
    for t in range(STEPS):
        y = alpha_ref[...] if t == 0 else y_ref[t - 1]
        ys_ref[t * ROWS : (t + 1) * ROWS] = (y.astype(F32) * inverse[t]).astype(BF16)
    for b in range(4):
        peers = slice(b * 16, (b + 1) * 16)
        v = jnp.concatenate(
            [
                wire_ref[peers, (STEPS + t) * PART : (STEPS + t + 1) * PART, :].reshape(256, ROWS)
                for t in range(STEPS)
            ],
            axis=1,
        )
        for ref, start in targets:
            ref[1, b * 256 : (b + 1) * 256, :] = dot(v, ys_ref[:, pl.ds(start, half)]).astype(BF16)

    loads[2].wait()
    loads[3].wait()
    f0, f1 = (factor_ref[t].astype(F32) for t in range(2))
    h = dot(turned_ref[...], jnp.concatenate([x_of(1), x_of(2)], axis=1))
    m_ref[:, ROWS : 2 * ROWS] = (h[:, :ROWS] * f0 * inv[1]).astype(BF16)
    h = dot(turned_ref[...], (h[:, ROWS:] * f0).astype(BF16)) * f1
    m_ref[:, 2 * ROWS :] = (h * inv[2]).astype(BF16)
    after_ref[...] = h.astype(BF16)
    loads[4].wait()
    for b in range(2):
        for ref, start in targets:
            at = pl.ds(pl.multiple_of(start + b * 256, 256), 256)
            value = dot_nt(weight_ref[...], m_ref[at, :])
            ref[0, :, b * 256 : (b + 1) * 256] = value.astype(BF16)


def alpha_kernel(after_ref, turned_ref, factor_ref, local_ref, total_ref, out_ref):
    inv = to_row(inverse_norm(total_ref[...], STEPS - 1))
    factor = factor_ref[STEPS - 1].astype(F32) * (local_ref[...] * inv)
    a = dot(turned_ref[...], after_ref[...]) * factor
    out_ref[...] = a.astype(BF16).reshape(PEERS, PART, ROWS)


def place(turn):
    x, y = lax.axis_index("dp"), lax.axis_index("y")
    return jnp.where((lax.axis_index("core") == 0) != turn, x, y)


def pair_kernel(keep_ref, got_ref, own_hbm, *refs):
    outs, own_ref, sem = [refs[3], *refs[:3]], refs[3], refs[4]
    along_dp = lax.axis_index("core") == 0
    me = place(False)
    for d in (2, 1, 3, 0):
        to = (me + d) & 3
        for b in range(4):
            row = jnp.where(along_dp, to * 256 + b * 64, b * 256 + to * 64)
            at = pl.ds(pl.multiple_of(row, 64), 64)
            for term in range(2):
                total = keep_ref[term, at, :].astype(F32) + got_ref[term, at, :].astype(F32)
                outs[d][term, b * 64 : (b + 1) * 64, :] = total.astype(BF16)
    own = pltpu.make_async_copy(own_ref, own_hbm, sem)
    own.start()
    own.wait()


def plane_kernel(own_hbm, *refs):
    others, outs, (sum_ref, own_ref, sem) = refs[:3], refs[3:7], refs[7:]
    own = pltpu.make_async_copy(own_hbm, own_ref, sem)
    own.start()
    me = place(True)
    sum_ref[...] = sum(r[...].astype(F32) for r in others)
    own.wait()
    sum_ref[...] += own_ref[...].astype(F32)
    for d in range(4):
        at = pl.ds(pl.multiple_of(((me + d) & 3) * 64, 64), 64)
        outs[d][...] = sum_ref[:, at, :].astype(BF16)


def line_kernel(*refs):
    ins, out_ref = refs[:4], refs[4]
    for term in range(2):
        total = sum(r[term].astype(F32) for r in ins)
        for n in range(16):
            out_ref[n, term * 4 : (term + 1) * 4, :] = total[n * 4 : (n + 1) * 4, :].astype(BF16)


def final_kernel(wire_ref, out_ref):
    def store(s, lanes, tile):
        out_ref[s * PART : (s + 1) * PART, lanes] = tile.astype(BF16)

    from_wire(wire_ref, 0, store)


def call(kernel, name, outs, scratch=(), flops=10**9, moved=8 * 10**6, limit=VMEM, specs=None):
    return pl.pallas_call(
        kernel,
        name=name,
        out_shape=[jax.ShapeDtypeStruct(s, d) for s, d in outs],
        scratch_shapes=[s if hasattr(s, "dtype") else pltpu.VMEM(*s) for s in scratch],
        compiler_params=pltpu.CompilerParams(vmem_limit_bytes=limit),
        cost_estimate=pl.CostEstimate(flops=flops, bytes_accessed=moved, transcendentals=0),
        **(specs or {}),
    )


def ring(x, d, turn):
    pairs = []
    for a in range(4):
        for b in range(4):
            for c in range(2):
                over_dp = (c == 0) != turn
                to = ((a + d) % 4, b) if over_dp else (a, (b + d) % 4)
                pairs.append(((a * 4 + b) * 2 + c, (to[0] * 4 + to[1]) * 2 + c))
    return lax.ppermute(x, ("dp", "y", "core"), pairs)


def in_hbm(*arrays):
    return [pltpu.with_memory_space_constraint(v, pltpu.HBM) for v in arrays]


def on_device(alpha_init, tokens, trans_rows, trans_cols, emit_rows, emit_cols, backward):
    alpha = alpha_init.reshape(ROWS, WIDTH)
    back = jnp.swapaxes(backward, 2, 3).reshape(STEPS, ROWS, WIDTH)
    tok = tokens.T
    half = WIDTH // 2
    state = ("y", "z", "core")

    hbm = pl.BlockSpec(memory_space=pltpu.HBM)
    wire_shape, y_shape = (PEERS, WIRE, ROWS), (STEPS - 1, ROWS, WIDTH)
    square, emit_shape = (WIDTH, WIDTH), emit_rows.shape
    wire, y = call(
        send_kernel, "send", [(wire_shape, BF16), (y_shape, BF16)],
        [
            ((ROWS, WIDTH), BF16), (square, BF16), (square, BF16), (emit_shape, BF16),
            (emit_shape, BF16), ((STEPS, ROWS, WIDTH), BF16), (wire_shape, BF16),
            (y_shape, BF16), ((ROWS, WIDTH), F32), ((STEPS * (ROWS + 8), WIDTH), BF16),
            ((2 * (ROWS + 8), WIDTH), BF16), pltpu.SemaphoreType.DMA((6,)),
            pltpu.SemaphoreType.DMA((8,)),
        ],
        limit=ALONE,
        specs=dict(
            in_specs=[pl.BlockSpec(memory_space=pltpu.VMEM)] + [hbm] * 6, out_specs=[hbm] * 2
        ),
    )(tok, alpha, trans_rows, trans_cols, emit_rows, emit_cols, back)
    got = lax.all_to_all(wire, state, 0, 0, tiled=True)

    weight, turned, factor, local, take_rows, take_cols = call(
        local_kernel, "local",
        [
            ((WIDTH, STEPS * ROWS), BF16), (square, BF16), ((STEPS, WIDTH, ROWS), BF16),
            ((1, ROWS), F32), ((8, WIDTH), F32), ((8, WIDTH), F32),
        ],
        limit=ALONE,
    )(tok, trans_rows, trans_cols, emit_rows, emit_cols, back)

    a_shape = (PEERS, PART, ROWS)
    vmem = pl.BlockSpec(memory_space=pltpu.VMEM)
    after, keep, give, total = call(
        counts_kernel, "counts",
        [
            ((WIDTH, ROWS), BF16), ((2, WIDTH, half), BF16), ((2, WIDTH, half), BF16),
            ((1, 128), F32),
        ],
        [
            (y_shape, BF16), ((ROWS, WIDTH), BF16), (square, BF16),
            ((STEPS, WIDTH, ROWS), BF16), ((WIDTH, STEPS * ROWS), BF16),
            ((STEPS * ROWS, WIDTH), BF16), ((WIDTH, STEPS * ROWS), BF16),
            pltpu.SemaphoreType.DMA((5,)),
        ],
        limit=40 * 2**20,
        specs=dict(in_specs=[vmem] + [hbm] * 5, out_specs=[vmem] * 4),
    )(got, *in_hbm(y, alpha, turned, factor, weight))
    (a_wire,) = call(alpha_kernel, "alpha", [(a_shape, BF16)])(
        after, *in_hbm(turned, factor, local), total
    )

    keep, a_wire = lax.optimization_barrier((keep, a_wire))

    core = lax.axis_index("core")
    swap_cores = [(0, 1), (1, 0)]
    shape, small = (2, 256, half), (2, 64, half)
    own, *pieces = call(
        pair_kernel, "pair", [(shape, BF16)] * 4, [(shape, BF16), pltpu.SemaphoreType.DMA(())],
        specs=dict(out_specs=[hbm] + [vmem] * 3),
    )(keep, lax.ppermute(give, "core", swap_cores))
    far, right, left = (ring(pieces[d - 1], d, False) for d in (2, 1, 3))
    mark, *_ = lax.optimization_barrier((total, *pieces))
    a_wire, _ = lax.optimization_barrier((a_wire, lax.ppermute(mark, "core", swap_cores)))
    a_got = lax.all_to_all(a_wire, state, 0, 0, tiled=True)
    own, *pieces = call(
        plane_kernel, "plane", [(small, BF16)] * 4,
        [(shape, F32), (shape, BF16), pltpu.SemaphoreType.DMA(())],
        specs=dict(in_specs=[hbm] + [vmem] * 3),
    )(*in_hbm(own), far, right, left)
    far, right, left = (ring(pieces[d - 1], d, True) for d in (2, 1, 3))
    (part,) = call(line_kernel, "line", [((16, 8, half), BF16)])(own, far, right, left)
    (alpha_final,) = call(final_kernel, "final", [((ROWS, WIDTH), BF16)])(a_got)
    part = lax.all_to_all(part, ("z", "core"), 0, 0, tiled=True)
    loglik = jnp.log(total[0, 2 : 3 * SEQ_DEV : 3] / (WIDTH * WIDTH))
    part, alpha_final, loglik = lax.optimization_barrier((part, alpha_final, loglik))
    sums = jnp.sum(part.reshape(8, 2, 2, 4, half).astype(F32), axis=0)
    sums = jnp.concatenate([sums[0], sums[1]], axis=2)
    scale = 1.0 / (SEQ_DEV * 4 * STEPS)
    counts_rows = sums[0] * take_rows[:4] * scale
    counts_cols = sums[1] * take_cols[:4] * scale

    return (
        alpha_final.reshape(SEQ_DEV, PART, WIDTH),
        counts_rows.T,
        counts_cols.T,
        loglik,
    )


def solution(mesh):
    mesh = jax.sharding.Mesh(mesh.devices.reshape(4, 4, 8, 2), ("dp", "y", "z", "core"))
    state = ("y", "z", "core")
    return jax.shard_map(
        on_device,
        mesh=mesh,
        in_specs=(
            P("dp", state, None),
            P("dp", None),
            P(),
            P(),
            P(),
            P(),
            P(None, "dp", None, state),
        ),
        out_specs=(
            P("dp", state, None),
            P(None, ("dp", *state)),
            P(None, ("dp", *state)),
            P("dp"),
        ),
        check_vma=False,
    )
```
